32 devices in a mesh: wide: 8 (over z, x), narrow: 4 (over y, core).
Axes of the slice: x: 2, y: 2, z: 4, core: 2. Of those that a mesh axis runs over, the one named last changes fastest.
Arguments:
- tokens: bfloat16 [16384, 768], P(('wide', 'narrow')), may hold values from -6 to 6
- cotangent: bfloat16 [16384, 768], P(('wide', 'narrow')), may hold values from -6 to 6
- segments: int32 [32, 512], P(('wide', 'narrow')), may hold values from 0 to 3, never falling along the last dimension, each value on 1 to 256 neighbouring positions
- buckets: int32 [512, 512], replicated, may hold values from 0 to 255
- norm1_gain: bfloat16 [768], P(('wide', 'narrow')), may hold values from 0.099609375 to 1.8984375
- norm1_bias: bfloat16 [768], P(('wide', 'narrow')), may hold values from -3 to 3
- qkv_weight: bfloat16 [768, 2304], P(('wide', 'narrow')), may hold values from -0.21875 to 0.21875
- qv_bias: bfloat16 [1536], P(('wide', 'narrow')), may hold values from -3 to 3
- head_scale: bfloat16 [12], replicated, may hold values from 0.5 to 2
- rel_table: bfloat16 [256, 12], P(('wide', 'narrow')), may hold values from -4 to 4
- out_weight: bfloat16 [768, 768], P(('wide', 'narrow')), may hold values from -0.21875 to 0.21875
- out_bias: bfloat16 [768], P(('wide', 'narrow')), may hold values from -3 to 3
- post_gain: bfloat16 [768], P(('wide', 'narrow')), may hold values from 0.099609375 to 1.8984375
- post_bias: bfloat16 [768], P(('wide', 'narrow')), may hold values from -3 to 3
- norm2_gain: bfloat16 [768], P(('wide', 'narrow')), may hold values from 0.099609375 to 1.8984375
- norm2_bias: bfloat16 [768], P(('wide', 'narrow')), may hold values from -3 to 3
- fc1_weight: bfloat16 [768, 3072], P(('wide', 'narrow')), may hold values from -0.21875 to 0.21875
- fc1_bias: bfloat16 [3072], P(('wide', 'narrow')), may hold values from -3 to 3
- inner_gain: bfloat16 [3072], P(('wide', 'narrow')), may hold values from 0.099609375 to 1.8984375
- inner_bias: bfloat16 [3072], P(('wide', 'narrow')), may hold values from -3 to 3
- fc2_weight: bfloat16 [3072, 768], P(('wide', 'narrow')), may hold values from -0.109375 to 0.109375
- fc2_bias: bfloat16 [768], P(('wide', 'narrow')), may hold values from -3 to 3
Outputs:
- output: bfloat16 [16384, 768], P(('wide', 'narrow'))
- grad_tokens: bfloat16 [16384, 768], P(('wide', 'narrow'))
- grad_norm1_gain: float32 [768], P(('wide', 'narrow'))
- grad_norm1_bias: float32 [768], P(('wide', 'narrow'))
- grad_qkv_weight: float32 [768, 2304], P(('wide', 'narrow'))
- grad_qv_bias: float32 [1536], P(('wide', 'narrow'))
- grad_head_scale: float32 [12], replicated
- grad_rel_table: float32 [256, 12], P(('wide', 'narrow'))
- grad_out_weight: float32 [768, 768], P(('wide', 'narrow'))
- grad_out_bias: float32 [768], P(('wide', 'narrow'))
- grad_post_gain: float32 [768], P(('wide', 'narrow'))
- grad_post_bias: float32 [768], P(('wide', 'narrow'))
- grad_norm2_gain: float32 [768], P(('wide', 'narrow'))
- grad_norm2_bias: float32 [768], P(('wide', 'narrow'))
- grad_fc1_weight: float32 [768, 3072], P(('wide', 'narrow'))
- grad_fc1_bias: float32 [3072], P(('wide', 'narrow'))
- grad_inner_gain: float32 [3072], P(('wide', 'narrow'))
- grad_inner_bias: float32 [3072], P(('wide', 'narrow'))
- grad_fc2_weight: float32 [3072, 768], P(('wide', 'narrow'))
- grad_fc2_bias: float32 [768], P(('wide', 'narrow'))
The draws below stay inside these ranges and needn't reach their ends.
Inputs may be any that keep to these rules, and one draw needn't show every extreme that they name: `segments`: segment numbers never fall along a row; each document has at most 256 tokens.
All inputs are finite; a program needn't handle non-finite values.
Results may differ from the reference program's by a relative error of at most 0.012.
Values may be sent and summed in bfloat16 or wider, within the bound.
A program may use at most 320 MiB of HBM per device.

```python
import math
import jax
import jax.numpy as jnp
import numpy as np
from jax import lax

D = 768
H = 12
FF = 3072
NB = 256
SEQ = 512
ROWS = 32
TOKENS = 16384


def with_ends(values, own_key, least, high):
    shape = values.shape
    place = [jax.random.randint(jax.random.fold_in(own_key, axis), (), 0, shape[axis]) for axis in range(len(shape))]
    values = values.at[tuple(place)].set(least)
    longest = shape.index(max(shape))
    place[longest] = (place[longest] + 1) % shape[longest]
    return values.at[tuple(place)].set(high)


def strengthened(values, key, source, target, blocks, factor):
    owner, partner = [(jnp.arange(values.shape[position]) // (values.shape[position] // blocks)).reshape([-1 if axis == position else 1 for axis in range(values.ndim)]) for position in (source, target)]
    chosen = jax.random.permutation(key, blocks)[partner]
    strong = (owner == chosen) | (owner == (partner + blocks // 2) % blocks)
    return jnp.where(strong, factor * values, values)


def steps_of(key, extent, pieces, low, top_value):
    level = 1.0
    for dim, blocks in pieces:
        steps = jax.random.uniform(jax.random.fold_in(jax.random.fold_in(key, 6), dim), (blocks,), jnp.float32, low / len(pieces), top_value / len(pieces))
        level = level * jnp.repeat(jnp.exp(steps), extent[dim] // blocks).reshape((-1,) + (1,) * (len(extent) - 1 - dim))
    return level


def split_up(amount, total, reach, lean):
    weights = [(1 << 20) // math.isqrt(standing ** lean) + 1 for standing in range(2, amount + 1)]
    rest, given = total - reach - (amount - 1), [1] * (amount - 1)
    while rest > 0:
        candidates = [i for i in range(amount - 1) if given[i] < reach]
        pool, budget = sum([weights[i] for i in candidates]), rest
        for i in candidates:
            addition = min(reach - given[i], max(1, budget * weights[i] // pool), rest)
            given[i] = given[i] + addition
            rest = rest - addition
    return np.array([reach] + given)


def ragged(rng, count, total, limit, slope):
    if count == 2:
        one = jax.random.randint(rng, (), max(1, total - limit), min(limit, total - 1) + 1)
        return jnp.stack([one, total - one])
    lengths = jnp.asarray(split_up(count, total, limit, slope), jnp.int32)
    couples = (count - 1) // 2
    donor, receiver = lengths[1:1 + 2 * couples:2], lengths[2:2 + 2 * couples:2]
    slack = jnp.minimum(donor - 1, limit - receiver)
    moved = jax.random.randint(jax.random.fold_in(rng, 1), (couples,), 0, 1 << 20) % (slack + 1)
    lengths = lengths.at[1:1 + 2 * couples:2].set(donor - moved).at[2:2 + 2 * couples:2].set(receiver + moved)
    return lengths[jax.random.permutation(jax.random.fold_in(rng, 2), count)]


def gaussian(own_key, extent, spread, bound, pieces=(), dtype=jnp.bfloat16):
    values = jax.random.normal(own_key, extent, jnp.float32) * spread
    if len(pieces) > 0:
        values = steps_of(own_key, extent, pieces, -0.22, 0.18) * values
    return jnp.clip(values, min=-bound, max=bound).astype(dtype)


def noise_with(stream_key, shape, scale, most, cuts, heavy, held_as=jnp.bfloat16):
    array = scale * jax.random.normal(stream_key, shape, jnp.float32)
    if cuts:
        array = array * steps_of(stream_key, shape, cuts, -0.22, 0.18)
    return jnp.clip(strengthened(array, jax.random.fold_in(stream_key, 3), *heavy), -most, most).astype(held_as)


def setup_inputs(seed: int = 0) -> dict:
    key_of = jax.random.split(jax.random.key(seed), 23)
    return {
        "tokens": gaussian(key_of[0], (TOKENS, D), 1.0, 6.0, ((0, 32),)),
        "cotangent": noise_with(key_of[1], (TOKENS, D), 1.0, 6.0, ((0, 32),), (0, 1, 32, 2.75)),
        "segments": jax.vmap(lambda own: jnp.searchsorted(jnp.cumsum(ragged(own, max(3, SEQ // 128), SEQ, SEQ // 2, 1)), jnp.arange(SEQ), side="right"))(jax.random.split(key_of[2], ROWS)).reshape((ROWS, SEQ)).astype(jnp.int32),
        "buckets": with_ends(jax.random.randint(key_of[3], (SEQ, SEQ), 0, NB), jax.random.fold_in(key_of[3], 1), 0, NB - 1).astype(jnp.int32),
        "norm1_gain": jnp.clip(1.0 + 0.18 * jax.random.normal(key_of[4], (D,), jnp.float32), 0.099609375, 1.8984375).astype(jnp.bfloat16),
        "norm1_bias": gaussian(key_of[5], (D,), 0.3, 3.0, ((0, 32),)),
        "qkv_weight": gaussian(key_of[6], (D, 3 * D), D ** -0.5, 0.21875, ((0, 32),)),
        "qv_bias": gaussian(key_of[7], (2 * D,), 0.5, 3.0, ((0, 32),)),
        "head_scale": jnp.clip(jnp.exp(jax.random.uniform(key_of[8], (H,), jnp.float32, math.log(0.5), math.log(2.0))), 0.5, 2.0).astype(jnp.bfloat16),
        "rel_table": gaussian(key_of[9], (NB, H), 1.0, 4.0, ((0, 32),)),
        "out_weight": gaussian(key_of[10], (D, D), D ** -0.5, 0.21875, ((0, 32),)),
        "out_bias": gaussian(key_of[11], (D,), 0.5, 3.0, ((0, 32),)),
        "post_gain": jnp.clip(1.0 + 0.18 * jax.random.normal(key_of[12], (D,), jnp.float32), 0.099609375, 1.8984375).astype(jnp.bfloat16),
        "post_bias": gaussian(key_of[13], (D,), 0.3, 3.0, ((0, 32),)),
        "norm2_gain": jnp.clip(1.0 + 0.18 * jax.random.normal(key_of[14], (D,), jnp.float32), 0.099609375, 1.8984375).astype(jnp.bfloat16),
        "norm2_bias": gaussian(key_of[15], (D,), 0.3, 3.0, ((0, 32),)),
        "fc1_weight": gaussian(key_of[16], (D, FF), D ** -0.5, 0.21875, ((0, 32),)),
        "fc1_bias": gaussian(key_of[17], (FF,), 0.5, 3.0, ((0, 32),)),
        "inner_gain": jnp.clip(1.0 + 0.18 * jax.random.normal(key_of[18], (FF,), jnp.float32), 0.099609375, 1.8984375).astype(jnp.bfloat16),
        "inner_bias": gaussian(key_of[19], (FF,), 0.3, 3.0, ((0, 32),)),
        "fc2_weight": gaussian(key_of[20], (FF, D), FF ** -0.5, 0.109375, ((0, 32),)),
        "fc2_bias": gaussian(key_of[21], (D,), 0.5, 3.0, ((0, 32),)),
    }


@jax.custom_vjp
def low(v):
    return lax.optimization_barrier(v.astype(jnp.bfloat16)).astype(jnp.float32)

@jax.custom_vjp
def low_back(v):
    return v

def low_keep(v):
    return (low(v), None)

def low_pass(kept, grad):
    return (grad,)

def back_keep(v):
    return (v, None)

def back_low(kept, grad):
    return (low(grad),)
low.defvjp(low_keep, low_pass)
low_back.defvjp(back_keep, back_low)

def standardize(v):
    centred = v - lax.optimization_barrier(jnp.mean(v, axis=-1, keepdims=True))
    return centred * lax.rsqrt(lax.optimization_barrier(jnp.mean(centred * centred, axis=-1, keepdims=True)) + 1e-05)

def matmul(left, right):
    return jnp.einsum('gsd,de->gse', left, right, precision=lax.Precision.HIGHEST)

def layer_group(params, xgroup, seggroup, buckets):
    norm1_gain, norm1_bias, qkv_weight, qv_bias, head_scale, rel_table, out_weight, out_bias, post_gain, post_bias, norm2_gain, norm2_bias, fc1_weight, fc1_bias, inner_gain, inner_bias, fc2_weight, fc2_bias = params
    group, seq, width = xgroup.shape
    heads = head_scale.shape[0]
    size = width // heads
    h1 = low(standardize(xgroup) * norm1_gain + norm1_bias)
    shift = jnp.concatenate([qv_bias[:width], jnp.zeros_like(qv_bias[:width]), qv_bias[width:]])
    qkv = low(low_back(matmul(h1, qkv_weight) + shift))
    query = qkv[:, :, :width].reshape(group, seq, heads, size)
    key = qkv[:, :, width:2 * width].reshape(group, seq, heads, size)
    value = qkv[:, :, 2 * width:].reshape(group, seq, heads, size)
    bias = jnp.transpose(rel_table[buckets], (2, 0, 1))
    scores = jnp.einsum('gqhd,gkhd->ghqk', query, key, precision=lax.Precision.HIGHEST) * 0.125 + bias[None]
    same = seggroup[:, :, None] == seggroup[:, None, :]
    scores = low_back(jnp.where(same[:, None], scores, -1000000000.0))
    probs = jax.nn.softmax(scores, axis=-1)
    attn = low_back(jnp.einsum('ghqk,gkhd->gqhd', low(probs), value, precision=lax.Precision.HIGHEST))
    scaled = low((attn * head_scale[None, None, :, None]).reshape(group, seq, width))
    mixed = low_back(matmul(scaled, out_weight) + out_bias)
    first = xgroup + standardize(mixed) * post_gain + post_bias
    h2 = low(standardize(first) * norm2_gain + norm2_bias)
    inner = low_back(matmul(h2, fc1_weight) + fc1_bias)
    hidden = low(standardize(jax.nn.gelu(inner, approximate=False)) * inner_gain + inner_bias)
    branch = low_back(matmul(hidden, fc2_weight) + fc2_bias)
    return first + branch

def reference(tokens, cotangent, segments, buckets, norm1_gain, norm1_bias, qkv_weight, qv_bias, head_scale, rel_table, out_weight, out_bias, post_gain, post_bias, norm2_gain, norm2_bias, fc1_weight, fc1_bias, inner_gain, inner_bias, fc2_weight, fc2_bias):
    params = tuple((w.astype(jnp.float32) for w in (norm1_gain, norm1_bias, qkv_weight, qv_bias, head_scale, rel_table, out_weight, out_bias, post_gain, post_bias, norm2_gain, norm2_bias, fc1_weight, fc1_bias, inner_gain, inner_bias, fc2_weight, fc2_bias)))
    group = math.gcd(ROWS, 8)
    xall = tokens.astype(jnp.float32).reshape(ROWS // group, group, SEQ, D)
    segall = segments.reshape(ROWS // group, group, SEQ)

    def forward(weights, inputs):

        def run(pair):
            return layer_group(weights, pair[0], pair[1], buckets)
        return lax.map(jax.checkpoint(run), (inputs, segall))
    result, pullback = jax.vjp(forward, params, xall)
    grads, grad_inputs = pullback(cotangent.astype(jnp.float32).reshape(ROWS // group, group, SEQ, D))
    output = result.reshape(TOKENS, D).astype(jnp.bfloat16)
    grad_tokens = grad_inputs.reshape(TOKENS, D).astype(jnp.bfloat16)
    return (output, grad_tokens, grads[0], grads[1], grads[2], grads[3], grads[4], grads[5], grads[6], grads[7], grads[8], grads[9], grads[10], grads[11], grads[12], grads[13], grads[14], grads[15], grads[16], grads[17])
```

```python
import functools
import math

import jax, jax.numpy as jnp
from jax import lax
from jax.experimental import pallas as pl
from jax.experimental.pallas import tpu as pltpu
from jax.sharding import PartitionSpec as P

f32 = jnp.float32
bf16 = jnp.bfloat16
NT = (((1,), (1,)), ((), ()))
TN = (((0,), (0,)), ((), ()))


def dot(a, b, dims=(((1,), (0,)), ((), ()))):
    return lax.dot_general(a, b, dims, preferred_element_type=f32)


def lookup(row, index):
    shape = index.shape
    low = jnp.broadcast_to(row[:, :128], shape)
    high = jnp.broadcast_to(row[:, 128:], shape)
    inner = index & 127
    return jnp.where(
        index < 128,
        jnp.take_along_axis(low, inner, axis=1),
        jnp.take_along_axis(high, inner, axis=1),
    )


def forward_kernel(q_ref, k_ref, v_ref, table_ref, buckets_ref, segc_ref, segr_ref,
                   attn_ref, p_ref):
    seq = q_ref.shape[0]
    pair = pl.program_id(0)
    even = lax.broadcasted_iota(jnp.int32, (1, 128), 1) < 64
    rows = 128
    for half in range(2):
        mine = even if half == 0 else jnp.logical_not(even)
        row = table_ref[0, half : half + 1, :]
        k = k_ref[...]
        v = v_ref[...]

        def body(step, carry):
            at = pl.ds(pl.multiple_of(step * rows, rows), rows)
            q = jnp.where(mine, q_ref[at, :], jnp.zeros((), bf16))
            raw = dot(q, k, NT) * 0.125
            bias = jnp.concatenate(
                [lookup(row, buckets_ref[at, pl.ds(128 * j, 128)]) for j in range(seq // 128)], axis=1
            )
            same = segc_ref[at, :] == segr_ref[...]
            scores = jnp.where(same, raw + bias, -1e9)
            top = jnp.max(scores, axis=1, keepdims=True)
            expo = jnp.exp(scores - top)
            total = jnp.sum(expo, axis=1, keepdims=True)
            probs = (expo * (1.0 / total)).astype(bf16)
            p_ref[half, at, :] = probs
            out = dot(probs, v)
            if half == 0:
                attn_ref[at, :] = out
            else:
                attn_ref[at, :] = jnp.where(even, attn_ref[at, :], out)
            return carry

        lax.fori_loop(0, seq // rows, body, 0)


def attention_forward(qkv, table_t, buckets, segments):
    seq, width = qkv.shape[0], qkv.shape[1] // 3
    pairs = width // 128
    nb = table_t.shape[2]
    return pl.pallas_call(
        forward_kernel,
        grid=(pairs,),
        in_specs=[
            pl.BlockSpec((seq, 128), lambda i: (0, i)),
            pl.BlockSpec((seq, 128), lambda i: (0, pairs + i)),
            pl.BlockSpec((seq, 128), lambda i: (0, 2 * pairs + i)),
            pl.BlockSpec((1, 2, nb), lambda i: (i, 0, 0)),
            pl.BlockSpec((seq, seq), lambda i: (0, 0)),
            pl.BlockSpec((seq, 1), lambda i: (0, 0)),
            pl.BlockSpec((1, seq), lambda i: (0, 0)),
        ],
        out_specs=[
            pl.BlockSpec((seq, 128), lambda i: (0, i)),
            pl.BlockSpec((2, seq, seq), lambda i: (i, 0, 0)),
        ],
        out_shape=[
            jax.ShapeDtypeStruct((seq, width), f32),
            jax.ShapeDtypeStruct((2 * pairs, seq, seq), bf16),
        ],
        name="attention_forward",
    )(qkv, qkv, qkv, table_t, buckets, segments.reshape(seq, 1), segments.reshape(1, seq))


HIGH = 4


def backward_kernel(q_ref, k_ref, v_ref, do_ref, attn_ref, p_ref, buckets_ref,
                    dq_ref, dk_ref, dv_ref, hist_ref, ds_ref, dst_ref, acc_ref):
    seq = q_ref.shape[0]
    heads = p_ref.shape[0] * pl.num_programs(0)
    pair = pl.program_id(0)
    even = lax.broadcasted_iota(jnp.int32, (1, 128), 1) < 64
    rows = 128
    chunks = seq // 128
    for half in range(2):
        mine = even if half == 0 else jnp.logical_not(even)
        k = k_ref[...]
        v = v_ref[...]
        head = pair * 2 + half

        def body(step, carry):
            at = pl.ds(pl.multiple_of(step * rows, rows), rows)
            do = jnp.where(mine, do_ref[at, :], jnp.zeros((), bf16))
            probs = p_ref[half, at, :]
            delta = jnp.sum(do.astype(f32) * attn_ref[at, :], axis=1, keepdims=True)
            ds = probs.astype(f32) * (dot(do, v, NT) - delta)
            for j in range(chunks):
                ds_ref[j, pl.ds(step * rows * 16 + head, rows, stride=16), :] = ds[:, 128 * j : 128 * j + 128]
            ds = ds.astype(bf16)
            dst_ref[at, :] = ds
            dq = dot(ds, k) * 0.125
            if half == 0:
                dq_ref[at, :] = dq.astype(bf16)
            else:
                dq_ref[at, :] = jnp.where(even, dq_ref[at, :], dq.astype(bf16))
            return carry

        lax.fori_loop(0, seq // rows, body, 0)
        dk = (dot(dst_ref[...], q_ref[...], TN) * 0.125).astype(bf16)
        dv = dot(p_ref[half], do_ref[...], TN).astype(bf16)
        if half == 0:
            dk_ref[...] = dk
            dv_ref[...] = dv
        else:
            dk_ref[...] = jnp.where(even, dk_ref[...], dk)
            dv_ref[...] = jnp.where(even, dv_ref[...], dv)

    @pl.when(pair == pl.num_programs(0) - 1)
    def _():
        acc_ref[...] = jnp.zeros_like(acc_ref)
        group = 8
        low = acc_ref.shape[1]

        def body(step, carry):
            base = pl.multiple_of(step * group, group)
            ids = buckets_ref[pl.ds(base, group), :]
            left, right = [], []
            for r in range(group):
                at = pl.ds(pl.multiple_of((base + r) * 16, 16), 16)
                d = jnp.concatenate([ds_ref[j, at, :] for j in range(chunks)], axis=1)
                idr = ids[r : r + 1, :]
                top = idr // low
                left.append(jnp.concatenate(
                    [jnp.where(top == b, d, 0.0) for b in range(HIGH)], axis=0).astype(bf16))
                which = lax.broadcasted_iota(jnp.int32, (low, seq), 0)
                right.append(jnp.where(which == (idr & (low - 1)), 1.0, 0.0).astype(bf16))
            acc_ref[...] += dot(jnp.concatenate(left, axis=1), jnp.concatenate(right, axis=1), NT)
            return carry

        lax.fori_loop(0, seq // group, body, 0)
        hist_ref[...] = acc_ref[...]


def attention_backward(qkv, d_attn, attn, p, buckets, nb):
    seq, width = d_attn.shape
    pairs = width // 128
    low = nb // HIGH
    narrow = lambda first: pl.BlockSpec((seq, 128), lambda i: (0, first + i))
    return pl.pallas_call(
        backward_kernel,
        grid=(pairs,),
        in_specs=[
            narrow(0), narrow(pairs), narrow(2 * pairs), narrow(0), narrow(0),
            pl.BlockSpec((2, seq, seq), lambda i: (i, 0, 0)),
            pl.BlockSpec((seq, seq), lambda i: (0, 0)),
        ],
        out_specs=[narrow(0), narrow(0), narrow(0), pl.BlockSpec((HIGH * 16, low), lambda i: (0, 0))],
        out_shape=[jax.ShapeDtypeStruct((seq, width), bf16)] * 3
        + [jax.ShapeDtypeStruct((HIGH * 16, low), f32)],
        scratch_shapes=[
            pltpu.VMEM((seq // 128, seq * 16, 128), f32),
            pltpu.VMEM((seq, seq), bf16),
            pltpu.VMEM((HIGH * 16, low), f32),
        ],
        name="attention_backward",
    )(qkv, qkv, qkv, d_attn, attn, p, buckets)


def table_gradient(hist, heads):
    high, low = HIGH, hist.shape[1]
    return hist.reshape(high, 16, low)[:, :heads].transpose(0, 2, 1).reshape(high * low, heads)

AXES = ("wide", "narrow")


def standardize(v):
    centred = v - jnp.mean(v, axis=-1, keepdims=True)
    inverse = lax.rsqrt(jnp.mean(centred * centred, axis=-1, keepdims=True) + 1e-05)
    return centred * inverse, inverse


def norm_back(grad, normed, inverse, gain):
    scaled = grad * gain
    return inverse * (
        scaled
        - jnp.mean(scaled, axis=-1, keepdims=True)
        - normed * jnp.mean(scaled * normed, axis=-1, keepdims=True)
    )


def pack(vectors, devices):
    return jnp.concatenate([v.reshape(devices, -1) for v in vectors], axis=1)


def unpack(packed, sizes):
    out, at = [], 0
    for size in sizes:
        out.append(packed[:, at : at + size].reshape(-1))
        at += size
    return out


def gather(x):
    return lax.all_gather(x, AXES, axis=0, tiled=True)


def scatter(x):
    return lax.psum_scatter(x, AXES, scatter_dimension=0, tiled=True)


def local(devices, tokens, cotangent, segments, buckets, norm1_gain, norm1_bias, qkv_weight, qv_bias,
          head_scale, rel_table, out_weight, out_bias, post_gain, post_bias, norm2_gain, norm2_bias,
          fc1_weight, fc1_bias, inner_gain, inner_bias, fc2_weight, fc2_bias):
    seq, width = tokens.shape
    heads = head_scale.shape[0]
    size = width // heads
    small = (norm1_gain, norm1_bias, out_bias, post_gain, post_bias, norm2_gain, norm2_bias, fc2_bias,
             qv_bias, fc1_bias, inner_gain, inner_bias, rel_table.reshape(-1))
    sizes = [v.shape[0] for v in small]
    nb = rel_table.shape[0] * devices
    packed = gather(jnp.concatenate(small)[None, :])
    w_qkv = gather(qkv_weight)
    w_out = gather(out_weight)
    w_first = gather(fc1_weight)
    w_second = gather(fc2_weight)
    (gain_one, bias_one, bias_out, gain_post, bias_post, gain_two, bias_two, bias_second,
     bias_qv, bias_first, gain_inner, bias_inner, table) = [v.astype(f32) for v in unpack(packed, sizes)]
    table_t = table.reshape(nb, heads).T.reshape(heads // 2, 2, nb)
    scale = jnp.repeat(head_scale.astype(f32), size)[None, :]

    inputs = tokens.astype(f32)
    hat_one, inv_one = standardize(inputs)
    h_one = (hat_one * gain_one + bias_one).astype(bf16)
    shift = jnp.concatenate([bias_qv[:width], jnp.zeros((width,), f32), bias_qv[width:]])
    qkv = (dot(h_one, w_qkv) + shift).astype(bf16)
    attn, probs = attention_forward(qkv, table_t, buckets, segments)
    scaled = (attn * scale).astype(bf16)
    mixed = dot(scaled, w_out) + bias_out
    hat_post, inv_post = standardize(mixed)
    first = inputs + hat_post * gain_post + bias_post
    hat_two, inv_two = standardize(first)
    h_two = (hat_two * gain_two + bias_two).astype(bf16)
    inner = dot(h_two, w_first) + bias_first
    cdf = 0.5 * (1.0 + lax.erf(inner * (1.0 / math.sqrt(2.0))))
    hat_inner, inv_inner = standardize(inner * cdf)
    hidden = (hat_inner * gain_inner + bias_inner).astype(bf16)
    output = (first + (dot(hidden, w_second) + bias_second)).astype(bf16)

    grad_out = cotangent.astype(f32)
    g_second = scatter(dot(hidden, cotangent, TN))
    g_second_bias = jnp.sum(grad_out, axis=0)
    d_hidden = dot(cotangent, w_second, NT)
    g_inner_gain = jnp.sum(d_hidden * hat_inner, axis=0)
    g_inner_bias = jnp.sum(d_hidden, axis=0)
    d_gelu = norm_back(d_hidden, hat_inner, inv_inner, gain_inner)
    pdf = jnp.exp(-0.5 * inner * inner) * (1.0 / math.sqrt(2.0 * math.pi))
    d_inner = (d_gelu * (cdf + inner * pdf)).astype(bf16)
    g_first_bias = jnp.sum(d_inner.astype(f32), axis=0)
    g_first = scatter(dot(h_two, d_inner, TN))
    d_two = dot(d_inner, w_first, NT)
    g_two_gain = jnp.sum(d_two * hat_two, axis=0)
    g_two_bias = jnp.sum(d_two, axis=0)
    d_first = grad_out + norm_back(d_two, hat_two, inv_two, gain_two)
    g_post_gain = jnp.sum(d_first * hat_post, axis=0)
    g_post_bias = jnp.sum(d_first, axis=0)
    d_mixed = norm_back(d_first, hat_post, inv_post, gain_post).astype(bf16)
    g_out_bias = jnp.sum(d_mixed.astype(f32), axis=0)
    g_out = scatter(dot(scaled, d_mixed, TN))
    d_scaled = dot(d_mixed, w_out, NT)
    g_scale = jnp.sum(jnp.sum(d_scaled * attn, axis=0).reshape(heads, size), axis=1)
    d_attn = (d_scaled * scale).astype(bf16)
    dq, dk, dv, hist = attention_backward(qkv, d_attn, attn, probs, buckets, nb)
    g_table = table_gradient(hist, heads)
    dqkv = jnp.concatenate([dq, dk, dv], axis=1)
    g_qv = jnp.concatenate([jnp.sum(dq.astype(f32), axis=0), jnp.sum(dv.astype(f32), axis=0)])
    g_qkv = scatter(dot(h_one, dqkv, TN))
    d_one = dot(dqkv, w_qkv, NT)
    g_one_gain = jnp.sum(d_one * hat_one, axis=0)
    g_one_bias = jnp.sum(d_one, axis=0)
    grad_tokens = (d_first + norm_back(d_one, hat_one, inv_one, gain_one)).astype(bf16)

    grads = (g_one_gain, g_one_bias, g_out_bias, g_post_gain, g_post_bias, g_two_gain, g_two_bias,
             g_second_bias, g_qv, g_first_bias, g_inner_gain, g_inner_bias, g_table.reshape(-1))
    summed = scatter(pack(grads, devices))
    g_scale = lax.psum(g_scale, AXES)
    (g_one_gain, g_one_bias, g_out_bias, g_post_gain, g_post_bias, g_two_gain, g_two_bias,
     g_second_bias, g_qv, g_first_bias, g_inner_gain, g_inner_bias, g_table) = unpack(summed, sizes)
    g_table = g_table.reshape(rel_table.shape)
    return (output, grad_tokens, g_one_gain, g_one_bias, g_qkv, g_qv, g_scale, g_table, g_out, g_out_bias,
            g_post_gain, g_post_bias, g_two_gain, g_two_bias, g_first, g_first_bias, g_inner_gain,
            g_inner_bias, g_second, g_second_bias)


def solution(mesh):
    devices = mesh.shape["wide"] * mesh.shape["narrow"]
    split, line, whole = P(AXES, None), P(AXES), P()
    return jax.shard_map(
        functools.partial(local, devices),
        mesh=mesh,
        in_specs=(split, split, split, whole, line, line, split, line, whole, split, split, line, line,
                  line, line, line, split, line, line, line, split, line),
        out_specs=(split, split, line, line, split, line, whole, split, split, line, line, line, line,
                   line, split, line, line, line, split, line),
        check_vma=False,
    )
```

```python
import functools
import math

import jax, jax.numpy as jnp
from jax import lax
from jax.experimental import pallas as pl
from jax.experimental.pallas import tpu as pltpu
from jax.sharding import PartitionSpec as P

f32 = jnp.float32
bf16 = jnp.bfloat16
NT = (((1,), (1,)), ((), ()))
TN = (((0,), (0,)), ((), ()))


def dot(a, b, dims=(((1,), (0,)), ((), ()))):
    return lax.dot_general(a, b, dims, preferred_element_type=f32)


def lookup(row, index):
    shape = index.shape
    low = jnp.broadcast_to(row[:, :128], shape)
    high = jnp.broadcast_to(row[:, 128:], shape)
    inner = index & 127
    return jnp.where(
        index < 128,
        jnp.take_along_axis(low, inner, axis=1),
        jnp.take_along_axis(high, inner, axis=1),
    )


def forward_kernel(q_ref, k_ref, v_ref, table_ref, buckets_ref, segc_ref, segr_ref,
                   attn_ref, p_ref):
    seq = q_ref.shape[0]
    pair = pl.program_id(0)
    even = lax.broadcasted_iota(jnp.int32, (1, 128), 1) < 64
    rows = 128
    for half in range(2):
        mine = even if half == 0 else jnp.logical_not(even)
        row = table_ref[0, half : half + 1, :]
        k = k_ref[...]
        v = v_ref[...]

        def body(step, carry):
            at = pl.ds(pl.multiple_of(step * rows, rows), rows)
            q = jnp.where(mine, q_ref[at, :], jnp.zeros((), bf16))
            raw = dot(q, k, NT) * 0.125
            bias = jnp.concatenate(
                [lookup(row, buckets_ref[at, pl.ds(128 * j, 128)]) for j in range(seq // 128)], axis=1
            )
            same = segc_ref[at, :] == segr_ref[...]
            scores = jnp.where(same, raw + bias, -1e9)
            top = jnp.max(scores, axis=1, keepdims=True)
            expo = jnp.exp(scores - top)
            total = jnp.sum(expo, axis=1, keepdims=True)
            probs = (expo * (1.0 / total)).astype(bf16)
            p_ref[half, at, :] = probs
            out = dot(probs, v)
            if half == 0:
                attn_ref[at, :] = out
            else:
                attn_ref[at, :] = jnp.where(even, attn_ref[at, :], out)
            return carry

        lax.fori_loop(0, seq // rows, body, 0)


def attention_forward(qkv, table_t, buckets, segments):
    seq, width = qkv.shape[0], qkv.shape[1] // 3
    pairs = width // 128
    nb = table_t.shape[2]
    return pl.pallas_call(
        forward_kernel,
        grid=(pairs,),
        in_specs=[
            pl.BlockSpec((seq, 128), lambda i: (0, i)),
            pl.BlockSpec((seq, 128), lambda i: (0, pairs + i)),
            pl.BlockSpec((seq, 128), lambda i: (0, 2 * pairs + i)),
            pl.BlockSpec((1, 2, nb), lambda i: (i, 0, 0)),
            pl.BlockSpec((seq, seq), lambda i: (0, 0)),
            pl.BlockSpec((seq, 1), lambda i: (0, 0)),
            pl.BlockSpec((1, seq), lambda i: (0, 0)),
        ],
        out_specs=[
            pl.BlockSpec((seq, 128), lambda i: (0, i)),
            pl.BlockSpec((2, seq, seq), lambda i: (i, 0, 0)),
        ],
        out_shape=[
            jax.ShapeDtypeStruct((seq, width), f32),
            jax.ShapeDtypeStruct((2 * pairs, seq, seq), bf16),
        ],
        name="attention_forward",
    )(qkv, qkv, qkv, table_t, buckets, segments.reshape(seq, 1), segments.reshape(1, seq))


HIGH = 4


def backward_kernel(q_ref, k_ref, v_ref, do_ref, attn_ref, p_ref, buckets_ref,
                    dq_ref, dk_ref, dv_ref, hist_ref, ds_ref, dst_ref, acc_ref):
    seq = q_ref.shape[0]
    heads = p_ref.shape[0] * pl.num_programs(0)
    pair = pl.program_id(0)
    even = lax.broadcasted_iota(jnp.int32, (1, 128), 1) < 64
    rows = 128
    chunks = seq // 128
    for half in range(2):
        mine = even if half == 0 else jnp.logical_not(even)
        k = k_ref[...]
        v = v_ref[...]
        head = pair * 2 + half

        def body(step, carry):
            at = pl.ds(pl.multiple_of(step * rows, rows), rows)
            do = jnp.where(mine, do_ref[at, :], jnp.zeros((), bf16))
            probs = p_ref[half, at, :]
            delta = jnp.sum(do.astype(f32) * attn_ref[at, :], axis=1, keepdims=True)
            ds = probs.astype(f32) * (dot(do, v, NT) - delta)
            for j in range(chunks):
                ds_ref[j, pl.ds(step * rows * 16 + head, rows, stride=16), :] = ds[:, 128 * j : 128 * j + 128]
            ds = ds.astype(bf16)
            dst_ref[at, :] = ds
            dq = dot(ds, k) * 0.125
            if half == 0:
                dq_ref[at, :] = dq.astype(bf16)
            else:
                dq_ref[at, :] = jnp.where(even, dq_ref[at, :], dq.astype(bf16))
            return carry

        lax.fori_loop(0, seq // rows, body, 0)
        dk = (dot(dst_ref[...], q_ref[...], TN) * 0.125).astype(bf16)
        dv = dot(p_ref[half], do_ref[...], TN).astype(bf16)
        if half == 0:
            dk_ref[...] = dk
            dv_ref[...] = dv
        else:
            dk_ref[...] = jnp.where(even, dk_ref[...], dk)
            dv_ref[...] = jnp.where(even, dv_ref[...], dv)

    @pl.when(pair == pl.num_programs(0) - 1)
    def _():
        acc_ref[...] = jnp.zeros_like(acc_ref)
        group = 8
        low = acc_ref.shape[1]

        def body(step, carry):
            base = pl.multiple_of(step * group, group)
            ids = buckets_ref[pl.ds(base, group), :]
            left, right = [], []
            for r in range(group):
                at = pl.ds(pl.multiple_of((base + r) * 16, 16), 16)
                d = jnp.concatenate([ds_ref[j, at, :] for j in range(chunks)], axis=1)
                idr = ids[r : r + 1, :]
                top = idr // low
                left.append(jnp.concatenate(
                    [jnp.where(top == b, d, 0.0) for b in range(HIGH)], axis=0).astype(bf16))
                which = lax.broadcasted_iota(jnp.int32, (low, seq), 0)
                right.append(jnp.where(which == (idr & (low - 1)), 1.0, 0.0).astype(bf16))
            acc_ref[...] += dot(jnp.concatenate(left, axis=1), jnp.concatenate(right, axis=1), NT)
            return carry

        lax.fori_loop(0, seq // group, body, 0)
        hist_ref[...] = acc_ref[...]


def attention_backward(qkv, d_attn, attn, p, buckets, nb):
    seq, width = d_attn.shape
    pairs = width // 128
    low = nb // HIGH
    narrow = lambda first: pl.BlockSpec((seq, 128), lambda i: (0, first + i))
    return pl.pallas_call(
        backward_kernel,
        grid=(pairs,),
        in_specs=[
            narrow(0), narrow(pairs), narrow(2 * pairs), narrow(0), narrow(0),
            pl.BlockSpec((2, seq, seq), lambda i: (i, 0, 0)),
            pl.BlockSpec((seq, seq), lambda i: (0, 0)),
        ],
        out_specs=[narrow(0), narrow(0), narrow(0), pl.BlockSpec((HIGH * 16, low), lambda i: (0, 0))],
        out_shape=[jax.ShapeDtypeStruct((seq, width), bf16)] * 3
        + [jax.ShapeDtypeStruct((HIGH * 16, low), f32)],
        scratch_shapes=[
            pltpu.VMEM((seq // 128, seq * 16, 128), f32),
            pltpu.VMEM((seq, seq), bf16),
            pltpu.VMEM((HIGH * 16, low), f32),
        ],
        name="attention_backward",
    )(qkv, qkv, qkv, d_attn, attn, p, buckets)


def table_gradient(hist, heads):
    high, low = HIGH, hist.shape[1]
    return hist.reshape(high, 16, low)[:, :heads].transpose(0, 2, 1).reshape(high * low, heads)

MESH = pl.DeviceIdType.MESH


class Place:
    def __init__(self):
        wide, narrow = lax.axis_index("wide"), lax.axis_index("narrow")
        self.z, self.x = wide // 2, wide % 2
        self.y, self.c = narrow // 2, narrow % 2

    def device(self, z=None, x=None, y=None, c=None):
        z = self.z if z is None else z
        x = self.x if x is None else x
        y = self.y if y is None else y
        c = self.c if c is None else c
        return (z * 2 + x, y * 2 + c)

    def peers(self):
        out = [self.device(z=(self.z + d) % 4) for d in (1, 2, 3)]
        return out + [self.device(x=1 - self.x), self.device(y=1 - self.y), self.device(c=1 - self.c)]

    def greet(self):
        barrier = pltpu.get_barrier_semaphore()
        for peer in self.peers():
            pl.semaphore_signal(barrier, inc=1, device_id=peer, device_id_type=MESH)
        pl.semaphore_wait(barrier, 6)


def send(src, dst, send_sem, recv_sem, to):
    copy = pltpu.make_async_remote_copy(
        src_ref=src, dst_ref=dst, send_sem=send_sem, recv_sem=recv_sem, device_id=to, device_id_type=MESH
    )
    copy.start()
    return copy


class Gather:
    SLOTS = 35

    def __init__(self, place, shard, whole, local_sem, send_sem, recv_sem):
        self.p, self.shard, self.whole = place, shard, whole
        self.local_sem, self.send_sem, self.recv_sem = local_sem, send_sem, recv_sem
        width = shard.shape[-1]
        self.half = (width // 256) * 128
        self.sent, self.width = [], width

    def at(self, z, x, y, c, part=None):
        ref = self.whole.at[z, x, y, c]
        if part == 0:
            return ref.at[:, pl.ds(0, self.half)]
        if part == 1:
            return ref.at[:, pl.ds(self.half, self.width - self.half)]
        return ref

    def go(self, src, dst, slot, to):
        self.sent.append(send(src, dst, self.send_sem.at[slot], self.recv_sem.at[slot], to))

    def arrived(self, dst, slot):
        pltpu.make_async_copy(dst, dst, self.recv_sem.at[slot]).wait()

    def begin(self):
        p = self.p
        mine = self.at(p.z, p.x, p.y, p.c)
        self.own = pltpu.make_async_copy(self.shard, mine, self.local_sem)
        self.own.start()
        for d in (1, 2, 3):
            self.go(self.shard, mine, d - 1, p.device(z=(p.z + d) % 4))
        self.go(self.shard, mine, 3, p.device(x=1 - p.x))
        self.go(self.shard, mine, 7, p.device(y=1 - p.y))
        self.go(self.shard, mine, 19, p.device(c=1 - p.c))

    def line(self):
        p = self.p
        for d in (1, 2, 3):
            ref = self.at((p.z + 4 - d) % 4, p.x, p.y, p.c)
            self.arrived(ref, d - 1)
            self.go(ref, ref, 3 + d, p.device(x=1 - p.x))
            self.go(ref, ref, 7 + d, p.device(y=1 - p.y))
            self.go(ref, ref, 19 + d, p.device(c=1 - p.c))

    def cross(self):
        p = self.p
        for d in range(4):
            z = (p.z + 4 - d) % 4
            ref = self.at(z, 1 - p.x, p.y, p.c)
            self.arrived(ref, 3 + d)
            if self.half:
                part = self.at(z, 1 - p.x, p.y, p.c, 0)
                self.go(part, part, 11 + d, p.device(y=1 - p.y))
            self.go(ref, ref, 23 + d, p.device(c=1 - p.c))
            ref = self.at(z, p.x, 1 - p.y, p.c)
            self.arrived(ref, 7 + d)
            part = self.at(z, p.x, 1 - p.y, p.c, 1)
            self.go(part, part, 15 + d, p.device(x=1 - p.x))
            self.go(ref, ref, 27 + d, p.device(c=1 - p.c))

    def corner(self):
        p = self.p
        for d in range(4):
            z = (p.z + 4 - d) % 4
            if self.half:
                self.arrived(self.at(z, 1 - p.x, 1 - p.y, p.c, 0), 11 + d)
            self.arrived(self.at(z, 1 - p.x, 1 - p.y, p.c, 1), 15 + d)
            ref = self.at(z, 1 - p.x, 1 - p.y, p.c)
            self.go(ref, ref, 31 + d, p.device(c=1 - p.c))

    def finish(self):
        p = self.p
        other = 1 - p.c
        for d in range(4):
            z = (p.z + 4 - d) % 4
            self.arrived(self.at(z, p.x, p.y, other), 19 + d)
            self.arrived(self.at(z, 1 - p.x, p.y, other), 23 + d)
            self.arrived(self.at(z, p.x, 1 - p.y, other), 27 + d)
            self.arrived(self.at(z, 1 - p.x, 1 - p.y, other), 31 + d)

    def drain(self):
        self.own.wait()
        for copy in self.sent:
            copy.wait_send()


def gather_kernel(count, *refs):
    shards, wholes = refs[:count], refs[count : 2 * count]
    local_sem, send_sem, recv_sem = refs[2 * count :]
    place = Place()
    place.greet()
    jobs = [
        Gather(place, shards[i], wholes[i], local_sem.at[i], send_sem.at[i], recv_sem.at[i])
        for i in range(count)
    ]
    for job in jobs:
        job.begin()
    for step in range(count + 2):
        if step < count:
            jobs[step].line()
        if 0 <= step - 1 < count:
            jobs[step - 1].cross()
        if 0 <= step - 2 < count:
            jobs[step - 2].corner()
    for job in jobs:
        job.finish()
    for job in jobs:
        job.drain()


def gather_all(shards, collective_id):
    count = len(shards)
    wholes = pl.pallas_call(
        functools.partial(gather_kernel, count),
        in_specs=[pl.BlockSpec(memory_space=pltpu.VMEM)] * count,
        out_specs=[pl.BlockSpec(memory_space=pl.ANY)] * count,
        out_shape=[jax.ShapeDtypeStruct((4, 2, 2, 2) + s.shape, s.dtype) for s in shards],
        scratch_shapes=[
            pltpu.SemaphoreType.DMA((count,)),
            pltpu.SemaphoreType.DMA((count, Gather.SLOTS)),
            pltpu.SemaphoreType.DMA((count, Gather.SLOTS)),
        ],
        compiler_params=pltpu.CompilerParams(collective_id=collective_id, has_side_effects=True),
        name="gather_all",
    )(*shards)
    return [w.reshape(32 * s.shape[0], s.shape[1]) for w, s in zip(wholes, shards)]


class Reduce:
    SLOTS = 12

    @staticmethod
    def scratch(shape, dtype):
        rows, width = shape
        half = (width // 256) * 128
        four = lambda w: pltpu.VMEM((4, rows, w), dtype)
        return [
            pltpu.VMEM((4, 4, rows, width), dtype),
            pltpu.VMEM((4, 4, rows, width), dtype),
            four(max(half, 128)), four(width - half), four(width), four(width),
            pltpu.VMEM((3, rows, width), dtype),
            pltpu.SemaphoreType.DMA((Reduce.SLOTS,)),
            pltpu.SemaphoreType.DMA((Reduce.SLOTS,)),
        ]

    def __init__(self, place, parts, out, scratch):
        self.p, self.parts, self.out = place, parts, out
        (self.other, self.ready, self.by_y, self.by_x, self.from_x, self.from_y, self.from_z,
         self.send_sem, self.recv_sem) = scratch
        width = out.shape[-1]
        self.half, self.width, self.sent = (width // 256) * 128, width, []

    def go(self, src, dst, slot, to):
        self.sent.append(send(src, dst, self.send_sem.at[slot], self.recv_sem.at[slot], to))

    def arrived(self, dst, slot):
        pltpu.make_async_copy(dst, dst, self.recv_sem.at[slot]).wait()

    def spots(self):
        p = self.p
        return [(1 - p.x, 1 - p.y), (1 - p.x, p.y), (p.x, 1 - p.y), (p.x, p.y)]

    def begin(self):
        p = self.p
        for i, (x, y) in enumerate(self.spots()):
            self.go(self.parts.at[:, x, y, 1 - p.c], self.other.at[i], i, p.device(c=1 - p.c))

    def pair(self, i, z):
        x, y = self.spots()[i]
        return self.parts[z, x, y, self.p.c].astype(f32) + self.other[i, z].astype(f32)

    def corner(self):
        p, half = self.p, self.half
        self.arrived(self.other.at[0], 0)

        @pl.loop(0, 4)
        def _(z):
            self.ready[0, z] = self.pair(0, z).astype(self.ready.dtype)

        if half:
            self.go(self.ready.at[0, :, :, pl.ds(0, half)], self.by_y, 4, p.device(y=1 - p.y))
        self.go(self.ready.at[0, :, :, pl.ds(half, self.width - half)], self.by_x, 5, p.device(x=1 - p.x))

    def cross(self):
        p, half = self.p, self.half
        self.arrived(self.other.at[1], 1)
        if half:
            self.arrived(self.by_y, 4)

        @pl.loop(0, 4)
        def _(z):
            total = self.pair(1, z)
            if half:
                total = jnp.concatenate([total[:, :half] + self.by_y[z].astype(f32), total[:, half:]], axis=1)
            self.ready[1, z] = total.astype(self.ready.dtype)

        self.go(self.ready.at[1], self.from_x, 6, p.device(x=1 - p.x))
        self.arrived(self.other.at[2], 2)
        self.arrived(self.by_x, 5)

        @pl.loop(0, 4)
        def _(z):
            total = self.pair(2, z)
            right = total[:, half:] + self.by_x[z].astype(f32)
            total = jnp.concatenate([total[:, :half], right], axis=1) if half else right
            self.ready[2, z] = total.astype(self.ready.dtype)

        self.go(self.ready.at[2], self.from_y, 7, p.device(y=1 - p.y))

    def line(self):
        p = self.p
        self.arrived(self.other.at[3], 3)
        self.arrived(self.from_x, 6)
        self.arrived(self.from_y, 7)
        for d in (1, 2, 3):
            z = (p.z + d) % 4
            total = self.pair(3, z) + self.from_x[z].astype(f32) + self.from_y[z].astype(f32)
            self.ready[3, z] = total.astype(self.ready.dtype)
            self.go(self.ready.at[3, z], self.from_z.at[d - 1], 7 + d, p.device(z=z))

    def finish(self):
        p = self.p
        for d in (1, 2, 3):
            self.arrived(self.from_z.at[d - 1], 7 + d)
        total = self.pair(3, p.z) + self.from_x[p.z].astype(f32) + self.from_y[p.z].astype(f32)
        for d in (1, 2, 3):
            total = total + self.from_z[d - 1].astype(f32)
        self.out[...] = total

    def drain(self):
        for copy in self.sent:
            copy.wait_send()


class Everywhere:
    @staticmethod
    def scratch(shape):
        return [pltpu.VMEM((3,) + shape, f32), pltpu.VMEM((6,) + shape, f32),
                pltpu.SemaphoreType.DMA((6,)), pltpu.SemaphoreType.DMA((6,))]

    def __init__(self, place, block, out, scratch):
        self.p, self.block, self.out, self.sent = place, block, out, []
        self.mine, self.got, self.send_sem, self.recv_sem = scratch

    def go(self, src, slot, to):
        self.sent.append(send(src, self.got.at[slot], self.send_sem.at[slot], self.recv_sem.at[slot], to))

    def arrived(self, slot):
        dst = self.got.at[slot]
        pltpu.make_async_copy(dst, dst, self.recv_sem.at[slot]).wait()

    def begin(self):
        self.go(self.block, 0, self.p.device(c=1 - self.p.c))

    def corner(self):
        self.arrived(0)
        self.mine[0] = self.block[...] + self.got[0]
        self.go(self.mine.at[0], 1, self.p.device(x=1 - self.p.x))

    def cross(self):
        self.arrived(1)
        self.mine[1] = self.mine[0] + self.got[1]
        self.go(self.mine.at[1], 2, self.p.device(y=1 - self.p.y))

    def line(self):
        p = self.p
        self.arrived(2)
        self.mine[2] = self.mine[1] + self.got[2]
        for d in (1, 2, 3):
            self.go(self.mine.at[2], 2 + d, p.device(z=(p.z + d) % 4))

    def finish(self):
        p = self.p
        for d in (1, 2, 3):
            self.arrived(2 + d)
        total = None
        for z in range(4):
            term = jnp.where(p.z == z, self.mine[2], 0.0)
            for d in (1, 2, 3):
                term = term + jnp.where((p.z + 4 - d) % 4 == z, self.got[2 + d], 0.0)
            total = term if total is None else total + term
        self.out[...] = total

    def drain(self):
        for copy in self.sent:
            copy.wait_send()


def reduce_kernel(count, extra, *refs):
    total = count + extra
    parts, outs, scratch = refs[:total], refs[total : 2 * total], refs[2 * total :]
    place = Place()
    place.greet()
    jobs = [Reduce(place, parts[i], outs[i], scratch[9 * i : 9 * i + 9]) for i in range(count)]
    if extra:
        jobs.append(Everywhere(place, parts[count], outs[count], scratch[9 * count :]))
    for job in jobs:
        job.begin()
    for step in range(total + 2):
        if step < total:
            jobs[step].corner()
        if 0 <= step - 1 < total:
            jobs[step - 1].cross()
        if 0 <= step - 2 < total:
            jobs[step - 2].line()
    for job in jobs:
        job.finish()
    for job in jobs:
        job.drain()


def reduce_all(parts, block, collective_id):
    shapes = [(p.shape[0] // 32, p.shape[1]) for p in parts]
    given = [p.reshape((4, 2, 2, 2) + s) for p, s in zip(parts, shapes)]
    outs = [jax.ShapeDtypeStruct(s, f32) for s in shapes]
    scratch = []
    for p, s in zip(parts, shapes):
        scratch += Reduce.scratch(s, p.dtype)
    extra = block is not None
    if extra:
        given.append(block)
        outs.append(jax.ShapeDtypeStruct(block.shape, f32))
        scratch += Everywhere.scratch(block.shape)
    return pl.pallas_call(
        functools.partial(reduce_kernel, len(parts), int(extra)),
        in_specs=[pl.BlockSpec(memory_space=pltpu.VMEM)] * len(given),
        out_specs=[pl.BlockSpec(memory_space=pltpu.VMEM)] * len(outs),
        out_shape=outs,
        scratch_shapes=scratch,
        compiler_params=pltpu.CompilerParams(
            collective_id=collective_id, has_side_effects=True, vmem_limit_bytes=60 * 2**20
        ),
        name="reduce_all",
    )(*given)

AXES = ("wide", "narrow")


def standardize(v):
    centred = v - jnp.mean(v, axis=-1, keepdims=True)
    inverse = lax.rsqrt(jnp.mean(centred * centred, axis=-1, keepdims=True) + 1e-05)
    return centred * inverse, inverse


def norm_back(grad, normed, inverse, gain):
    scaled = grad * gain
    return inverse * (
        scaled
        - jnp.mean(scaled, axis=-1, keepdims=True)
        - normed * jnp.mean(scaled * normed, axis=-1, keepdims=True)
    )


def pack(vectors, devices):
    return jnp.concatenate([v.reshape(devices, -1) for v in vectors], axis=1)


def unpack(packed, sizes):
    out, at = [], 0
    for size in sizes:
        out.append(packed[:, at : at + size].reshape(-1))
        at += size
    return out


def fill(x, count):
    return jnp.pad(x, ((0, 0), (0, count - x.shape[1])))


class Plain:
    held = f32

    @staticmethod
    def gather(shards, small):
        return [lax.all_gather(x, AXES, axis=0, tiled=True) for x in (*shards, small)]

    @staticmethod
    def reduce(parts, small, block):
        sums = [lax.psum_scatter(x, AXES, scatter_dimension=0, tiled=True) for x in (*parts, small)]
        return sums, lax.psum(block, AXES)


class Direct:
    held = bf16

    @staticmethod
    def gather(shards, small):
        tiles = fill(small, 1024).reshape(8, 128)
        *wholes, tiles = gather_all([*shards, tiles], 0)
        return [*wholes, tiles.reshape(32, 1024)]

    @staticmethod
    def reduce(parts, small, block):
        tiles = fill(small, 1024).reshape(256, 128)
        line = fill(block[None, :], 1024).reshape(8, 128)
        *sums, tiles, line = reduce_all([*parts, tiles], line, 1)
        return [*sums, tiles.reshape(1, 1024)], line.reshape(-1)[: block.shape[0]]


def local(devices, ways, tokens, cotangent, segments, buckets, norm1_gain, norm1_bias, qkv_weight, qv_bias,
          head_scale, rel_table, out_weight, out_bias, post_gain, post_bias, norm2_gain, norm2_bias,
          fc1_weight, fc1_bias, inner_gain, inner_bias, fc2_weight, fc2_bias):
    seq, width = tokens.shape
    heads = head_scale.shape[0]
    size = width // heads
    small = (norm1_gain, norm1_bias, out_bias, post_gain, post_bias, norm2_gain, norm2_bias, fc2_bias,
             qv_bias, fc1_bias, inner_gain, inner_bias, rel_table.reshape(-1))
    sizes = [v.shape[0] for v in small]
    nb = rel_table.shape[0] * devices
    w_qkv, w_out, w_first, w_second, packed = ways.gather(
        (qkv_weight, out_weight, fc1_weight, fc2_weight), jnp.concatenate(small)[None, :])
    (gain_one, bias_one, bias_out, gain_post, bias_post, gain_two, bias_two, bias_second,
     bias_qv, bias_first, gain_inner, bias_inner, table) = [v.astype(f32) for v in unpack(packed, sizes)]
    table_t = table.reshape(nb, heads).T.reshape(heads // 2, 2, nb)
    scale = jnp.repeat(head_scale.astype(f32), size)[None, :]

    inputs = tokens.astype(f32)
    hat_one, inv_one = standardize(inputs)
    h_one = (hat_one * gain_one + bias_one).astype(bf16)
    shift = jnp.concatenate([bias_qv[:width], jnp.zeros((width,), f32), bias_qv[width:]])
    qkv = (dot(h_one, w_qkv) + shift).astype(bf16)
    attn, probs = attention_forward(qkv, table_t, buckets, segments)
    scaled = (attn * scale).astype(bf16)
    mixed = dot(scaled, w_out) + bias_out
    hat_post, inv_post = standardize(mixed)
    first = inputs + hat_post * gain_post + bias_post
    hat_two, inv_two = standardize(first)
    h_two = (hat_two * gain_two + bias_two).astype(bf16)
    inner = dot(h_two, w_first) + bias_first
    cdf = 0.5 * (1.0 + lax.erf(inner * (1.0 / math.sqrt(2.0))))
    hat_inner, inv_inner = standardize(inner * cdf)
    hidden = (hat_inner * gain_inner + bias_inner).astype(bf16)
    output = (first + (dot(hidden, w_second) + bias_second)).astype(bf16)

    grad_out = cotangent.astype(f32)
    g_second = dot(hidden, cotangent, TN).astype(ways.held)
    g_second_bias = jnp.sum(grad_out, axis=0)
    d_hidden = dot(cotangent, w_second, NT)
    g_inner_gain = jnp.sum(d_hidden * hat_inner, axis=0)
    g_inner_bias = jnp.sum(d_hidden, axis=0)
    d_gelu = norm_back(d_hidden, hat_inner, inv_inner, gain_inner)
    pdf = jnp.exp(-0.5 * inner * inner) * (1.0 / math.sqrt(2.0 * math.pi))
    d_inner = (d_gelu * (cdf + inner * pdf)).astype(bf16)
    g_first_bias = jnp.sum(d_inner.astype(f32), axis=0)
    g_first = dot(h_two, d_inner, TN).astype(ways.held)
    d_two = dot(d_inner, w_first, NT)
    g_two_gain = jnp.sum(d_two * hat_two, axis=0)
    g_two_bias = jnp.sum(d_two, axis=0)
    d_first = grad_out + norm_back(d_two, hat_two, inv_two, gain_two)
    g_post_gain = jnp.sum(d_first * hat_post, axis=0)
    g_post_bias = jnp.sum(d_first, axis=0)
    d_mixed = norm_back(d_first, hat_post, inv_post, gain_post).astype(bf16)
    g_out_bias = jnp.sum(d_mixed.astype(f32), axis=0)
    g_out = dot(scaled, d_mixed, TN).astype(ways.held)
    d_scaled = dot(d_mixed, w_out, NT)
    g_scale = jnp.sum(jnp.sum(d_scaled * attn, axis=0).reshape(heads, size), axis=1)
    d_attn = (d_scaled * scale).astype(bf16)
    dq, dk, dv, hist = attention_backward(qkv, d_attn, attn, probs, buckets, nb)
    g_table = table_gradient(hist, heads)
    dqkv = jnp.concatenate([dq, dk, dv], axis=1)
    g_qv = jnp.concatenate([jnp.sum(dq.astype(f32), axis=0), jnp.sum(dv.astype(f32), axis=0)])
    g_qkv = dot(h_one, dqkv, TN).astype(ways.held)
    d_one = dot(dqkv, w_qkv, NT)
    g_one_gain = jnp.sum(d_one * hat_one, axis=0)
    g_one_bias = jnp.sum(d_one, axis=0)
    grad_tokens = (d_first + norm_back(d_one, hat_one, inv_one, gain_one)).astype(bf16)

    grads = (g_one_gain, g_one_bias, g_out_bias, g_post_gain, g_post_bias, g_two_gain, g_two_bias,
             g_second_bias, g_qv, g_first_bias, g_inner_gain, g_inner_bias, g_table.reshape(-1))
    (g_qkv, g_out, g_first, g_second, summed), g_scale = ways.reduce(
        (g_qkv, g_out, g_first, g_second), pack(grads, devices), g_scale)
    (g_one_gain, g_one_bias, g_out_bias, g_post_gain, g_post_bias, g_two_gain, g_two_bias,
     g_second_bias, g_qv, g_first_bias, g_inner_gain, g_inner_bias, g_table) = unpack(summed, sizes)
    g_table = g_table.reshape(rel_table.shape)
    return (output, grad_tokens, g_one_gain, g_one_bias, g_qkv, g_qv, g_scale, g_table, g_out, g_out_bias,
            g_post_gain, g_post_bias, g_two_gain, g_two_bias, g_first, g_first_bias, g_inner_gain,
            g_inner_bias, g_second, g_second_bias)


def solution(mesh):
    devices = mesh.shape["wide"] * mesh.shape["narrow"]
    direct = (mesh.shape["wide"], mesh.shape["narrow"]) == (8, 4)
    split, line, whole = P(AXES, None), P(AXES), P()
    return jax.shard_map(
        functools.partial(local, devices, Direct if direct else Plain),
        mesh=mesh,
        in_specs=(split, split, split, whole, line, line, split, line, whole, split, split, line, line,
                  line, line, line, split, line, line, line, split, line),
        out_specs=(split, split, line, line, split, line, whole, split, split, line, line, line, line,
                   line, split, line, line, line, split, line),
        check_vma=False,
    )
```

```python
import functools
import math

import jax, jax.numpy as jnp
from jax import lax
from jax.experimental import pallas as pl
from jax.experimental.pallas import tpu as pltpu
from jax.sharding import PartitionSpec as P

f32 = jnp.float32
bf16 = jnp.bfloat16
NT = (((1,), (1,)), ((), ()))
TN = (((0,), (0,)), ((), ()))


def dot(a, b, dims=(((1,), (0,)), ((), ()))):
    return lax.dot_general(a, b, dims, preferred_element_type=f32)


def lookup(row, index):
    shape = index.shape
    low = jnp.broadcast_to(row[:, :128], shape)
    high = jnp.broadcast_to(row[:, 128:], shape)
    inner = index & 127
    return jnp.where(
        index < 128,
        jnp.take_along_axis(low, inner, axis=1),
        jnp.take_along_axis(high, inner, axis=1),
    )


def forward_half(half, q_ref, k_ref, v_ref, table_ref, buckets_ref, segc_ref, segr_ref, attn_ref, p_ref):
    seq = q_ref.shape[0]
    even = lax.broadcasted_iota(jnp.int32, (1, 128), 1) < 64
    mine = even if half == 0 else jnp.logical_not(even)
    rows = 128
    row = table_ref[0, half : half + 1, :]
    k = k_ref[...]
    v = v_ref[...]

    def body(step, carry):
        at = pl.ds(pl.multiple_of(step * rows, rows), rows)
        q = jnp.where(mine, q_ref[at, :], jnp.zeros((), bf16))
        raw = dot(q, k, NT) * 0.125
        bias = jnp.concatenate(
            [lookup(row, buckets_ref[at, pl.ds(128 * j, 128)]) for j in range(seq // 128)], axis=1
        )
        same = segc_ref[at, :] == segr_ref[...]
        scores = jnp.where(same, raw + bias, -1e9)
        top = jnp.max(scores, axis=1, keepdims=True)
        expo = jnp.exp(scores - top)
        total = jnp.sum(expo, axis=1, keepdims=True)
        probs = (expo * (1.0 / total)).astype(bf16)
        p_ref[half, at, :] = probs
        out = dot(probs, v)
        if half == 0:
            attn_ref[at, :] = out
        else:
            attn_ref[at, :] = jnp.where(even, attn_ref[at, :], out)
        return carry

    lax.fori_loop(0, seq // rows, body, 0)


def forward_kernel(*refs):
    for half in range(2):
        forward_half(half, *refs)


def spread(steps, first, slots):
    plan = [[] for _ in range(slots)]
    plan[0] += first
    for i, step in enumerate(steps):
        plan[1 + i * (slots - 1) // len(steps)].append(step)
    return plan


def run_at(where, plan):
    for k, steps in enumerate(plan):
        if steps:

            @pl.when(where == k)
            def _():
                for step in steps:
                    step()


def forward_gather_kernel(count, pairs, *refs):
    ins, shards, outs = refs[:7], refs[7 : 7 + count], refs[7 + count : 9 + count]
    wholes = refs[9 + count : 9 + 2 * count]
    local_sem, send_sem, recv_sem = refs[9 + 2 * count :]
    place = Place()
    jobs = [
        Gather(place, shards[i], wholes[i], local_sem.at[i], send_sem.at[i], recv_sem.at[i])
        for i in range(count)
    ]
    plan = spread(gather_steps(jobs), [place.greet] + [job.begin for job in jobs], 2 * pairs)
    pair = pl.program_id(0)
    for half in range(2):
        run_at(pair, plan[half::2])
        forward_half(half, *ins, *outs)
    run_at(pair, [[]] * (pairs - 1) + [[job.finish for job in jobs] + [job.drain for job in jobs]])


def attention_forward(qkv, table_t, buckets, segments, shards=()):
    seq, width = qkv.shape[0], qkv.shape[1] // 3
    pairs = width // 128
    nb = table_t.shape[2]
    count = len(shards)
    kernel, scratch, params = forward_kernel, [], None
    if count:
        kernel = functools.partial(forward_gather_kernel, count, pairs)
        scratch = gather_scratch(count)
        params = pltpu.CompilerParams(collective_id=2, has_side_effects=True)
    attn, probs, *wholes = pl.pallas_call(
        kernel,
        grid=(pairs,),
        in_specs=[
            pl.BlockSpec((seq, 128), lambda i: (0, i)),
            pl.BlockSpec((seq, 128), lambda i: (0, pairs + i)),
            pl.BlockSpec((seq, 128), lambda i: (0, 2 * pairs + i)),
            pl.BlockSpec((1, 2, nb), lambda i: (i, 0, 0)),
            pl.BlockSpec((seq, seq), lambda i: (0, 0)),
            pl.BlockSpec((seq, 1), lambda i: (0, 0)),
            pl.BlockSpec((1, seq), lambda i: (0, 0)),
        ]
        + [pl.BlockSpec(memory_space=pltpu.VMEM)] * count,
        out_specs=[
            pl.BlockSpec((seq, 128), lambda i: (0, i)),
            pl.BlockSpec((2, seq, seq), lambda i: (i, 0, 0)),
        ]
        + [pl.BlockSpec(memory_space=pl.ANY)] * count,
        out_shape=[
            jax.ShapeDtypeStruct((seq, width), f32),
            jax.ShapeDtypeStruct((2 * pairs, seq, seq), bf16),
        ]
        + [whole_shape(x) for x in shards],
        scratch_shapes=scratch,
        compiler_params=params,
        name="attention_forward",
    )(qkv, qkv, qkv, table_t, buckets, segments.reshape(seq, 1), segments.reshape(1, seq), *shards)
    return attn, probs, [w.reshape(32 * x.shape[0], x.shape[1]) for w, x in zip(wholes, shards)]


HIGH = 4


def backward_half(half, pair, q_ref, k_ref, v_ref, do_ref, attn_ref, p_ref, dq_ref, dk_ref, dv_ref, ds_ref, dst_ref):
    seq = q_ref.shape[0]
    even = lax.broadcasted_iota(jnp.int32, (1, 128), 1) < 64
    mine = even if half == 0 else jnp.logical_not(even)
    rows = 128
    chunks = seq // 128
    k = k_ref[...]
    v = v_ref[...]
    head = pair * 2 + half

    def body(step, carry):
        at = pl.ds(pl.multiple_of(step * rows, rows), rows)
        do = jnp.where(mine, do_ref[at, :], jnp.zeros((), bf16))
        probs = p_ref[half, at, :]
        delta = jnp.sum(do.astype(f32) * attn_ref[at, :], axis=1, keepdims=True)
        ds = probs.astype(f32) * (dot(do, v, NT) - delta)
        for j in range(chunks):
            ds_ref[j, pl.ds(step * rows * 16 + head, rows, stride=16), :] = ds[:, 128 * j : 128 * j + 128]
        ds = ds.astype(bf16)
        dst_ref[at, :] = ds
        dq = dot(ds, k) * 0.125
        if half == 0:
            dq_ref[at, :] = dq.astype(bf16)
        else:
            dq_ref[at, :] = jnp.where(even, dq_ref[at, :], dq.astype(bf16))
        return carry

    lax.fori_loop(0, seq // rows, body, 0)
    dk = (dot(dst_ref[...], q_ref[...], TN) * 0.125).astype(bf16)
    dv = dot(p_ref[half], do_ref[...], TN).astype(bf16)
    if half == 0:
        dk_ref[...] = dk
        dv_ref[...] = dv
    else:
        dk_ref[...] = jnp.where(even, dk_ref[...], dk)
        dv_ref[...] = jnp.where(even, dv_ref[...], dv)


def histogram(part, parts, buckets_ref, ds_ref, acc_ref):
    seq = buckets_ref.shape[0]
    chunks = seq // 128
    group = 8
    low = acc_ref.shape[1]

    def body(step, carry):
        base = pl.multiple_of(step * group, group)
        ids = buckets_ref[pl.ds(base, group), :]
        left, right = [], []
        for r in range(group):
            at = pl.ds(pl.multiple_of((base + r) * 16, 16), 16)
            d = jnp.concatenate([ds_ref[j, at, :] for j in range(chunks)], axis=1)
            idr = ids[r : r + 1, :]
            top = idr // low
            left.append(jnp.concatenate([jnp.where(top == b, d, 0.0) for b in range(HIGH)], axis=0).astype(bf16))
            which = lax.broadcasted_iota(jnp.int32, (low, seq), 0)
            right.append(jnp.where(which == (idr & (low - 1)), 1.0, 0.0).astype(bf16))
        acc_ref[...] += dot(jnp.concatenate(left, axis=1), jnp.concatenate(right, axis=1), NT)
        return carry

    steps = seq // group // parts
    lax.fori_loop(part * steps, (part + 1) * steps, body, 0)


PARTS = 4


def backward_kernel(count, *refs):
    ins, buckets_ref, parts = refs[:6], refs[6], refs[7 : 7 + count]
    outs, hist_ref, sums = refs[7 + count : 10 + count], refs[10 + count], refs[11 + count : 11 + 2 * count]
    ds_ref, dst_ref, acc_ref, *scratch = refs[11 + 2 * count :]
    pair = pl.program_id(0)
    pairs = 6 if count else None
    if count:
        place = Place()
        jobs = [Reduce(place, parts[i], sums[i], scratch[9 * i : 9 * i + 9]) for i in range(count)]
        plan = spread(reduce_steps(jobs), [place.greet] + [job.begin for job in jobs], 2 * pairs + PARTS)

    @pl.when(pair == 0)
    def _():
        acc_ref[...] = jnp.zeros_like(acc_ref)

    for half in range(2):
        if count:
            run_at(pair, plan[half : 2 * pairs : 2])
        backward_half(half, pair, *ins, *outs, ds_ref, dst_ref)

    @pl.when(pair == pl.num_programs(0) - 1)
    def _():
        for part in range(PARTS):
            if count:
                for step in plan[2 * pairs + part]:
                    step()
            histogram(part, PARTS, buckets_ref, ds_ref, acc_ref)
        hist_ref[...] = acc_ref[...]
        if count:
            for job in jobs:
                job.finish()
            for job in jobs:
                job.drain()


def attention_backward(qkv, d_attn, attn, p, buckets, nb, parts=()):
    seq, width = d_attn.shape
    pairs = width // 128
    low = nb // HIGH
    count = len(parts)
    narrow = lambda first: pl.BlockSpec((seq, 128), lambda i: (0, first + i))
    scratch, params, shapes = [], None, []
    if count:
        shapes = [(x.shape[0] // 32, x.shape[1]) for x in parts]
        for x, shape in zip(parts, shapes):
            scratch += Reduce.scratch(shape, x.dtype)
        parts = [x.reshape((4, 2, 2, 2) + shape) for x, shape in zip(parts, shapes)]
        params = pltpu.CompilerParams(collective_id=3, has_side_effects=True, vmem_limit_bytes=63 * 2**20)
    dq, dk, dv, hist, *sums = pl.pallas_call(
        functools.partial(backward_kernel, count),
        grid=(pairs,),
        in_specs=[
            narrow(0), narrow(pairs), narrow(2 * pairs), narrow(0), narrow(0),
            pl.BlockSpec((2, seq, seq), lambda i: (i, 0, 0)),
            pl.BlockSpec((seq, seq), lambda i: (0, 0), pipeline_mode=pl.Buffered(1)),
        ]
        + [pl.BlockSpec(memory_space=pltpu.VMEM)] * count,
        out_specs=[narrow(0), narrow(0), narrow(0), pl.BlockSpec((HIGH * 16, low), lambda i: (0, 0))]
        + [pl.BlockSpec(memory_space=pltpu.VMEM)] * count,
        out_shape=[jax.ShapeDtypeStruct((seq, width), bf16)] * 3
        + [jax.ShapeDtypeStruct((HIGH * 16, low), f32)]
        + [jax.ShapeDtypeStruct(shape, f32) for shape in shapes],
        scratch_shapes=[
            pltpu.VMEM((seq // 128, seq * 16, 128), f32),
            pltpu.VMEM((seq, seq), bf16),
            pltpu.VMEM((HIGH * 16, low), f32),
        ]
        + scratch,
        compiler_params=params,
        name="attention_backward",
    )(qkv, qkv, qkv, d_attn, attn, p, buckets, *parts)
    return dq, dk, dv, hist, sums


def table_gradient(hist, heads):
    high, low = HIGH, hist.shape[1]
    return hist.reshape(high, 16, low)[:, :heads].transpose(0, 2, 1).reshape(high * low, heads)

MESH = pl.DeviceIdType.MESH


class Place:
    def __init__(self):
        wide, narrow = lax.axis_index("wide"), lax.axis_index("narrow")
        self.z, self.x = wide // 2, wide % 2
        self.y, self.c = narrow // 2, narrow % 2

    def device(self, z=None, x=None, y=None, c=None):
        z = self.z if z is None else z
        x = self.x if x is None else x
        y = self.y if y is None else y
        c = self.c if c is None else c
        return (z * 2 + x, y * 2 + c)

    def peers(self):
        out = [self.device(z=(self.z + d) % 4) for d in (1, 2, 3)]
        return out + [self.device(x=1 - self.x), self.device(y=1 - self.y), self.device(c=1 - self.c)]

    def greet(self):
        barrier = pltpu.get_barrier_semaphore()
        for peer in self.peers():
            pl.semaphore_signal(barrier, inc=1, device_id=peer, device_id_type=MESH)
        pl.semaphore_wait(barrier, 6)


def send(src, dst, send_sem, recv_sem, to):
    copy = pltpu.make_async_remote_copy(
        src_ref=src, dst_ref=dst, send_sem=send_sem, recv_sem=recv_sem, device_id=to, device_id_type=MESH
    )
    copy.start()
    return copy


class Gather:
    SLOTS = 35

    def __init__(self, place, shard, whole, local_sem, send_sem, recv_sem):
        self.p, self.shard, self.whole = place, shard, whole
        self.local_sem, self.send_sem, self.recv_sem = local_sem, send_sem, recv_sem
        self.width = shard.shape[-1]
        self.half = (self.width // 256) * 128

    def at(self, z, x, y, c, part=None):
        ref = self.whole.at[z, x, y, c]
        if part == 0:
            return ref.at[:, pl.ds(0, self.half)]
        if part == 1:
            return ref.at[:, pl.ds(self.half, self.width - self.half)]
        return ref

    def go(self, src, dst, slot, to):
        send(src, dst, self.send_sem.at[slot], self.recv_sem.at[slot], to)

    def arrived(self, dst, slot):
        pltpu.make_async_copy(dst, dst, self.recv_sem.at[slot]).wait()

    def begin(self):
        p = self.p
        mine = self.at(p.z, p.x, p.y, p.c)
        pltpu.make_async_copy(self.shard, mine, self.local_sem).start()
        for d in (1, 2, 3):
            self.go(self.shard, mine, d - 1, p.device(z=(p.z + d) % 4))
        self.go(self.shard, mine, 3, p.device(x=1 - p.x))
        self.go(self.shard, mine, 7, p.device(y=1 - p.y))
        self.go(self.shard, mine, 19, p.device(c=1 - p.c))

    def line(self, d):
        p = self.p
        ref = self.at((p.z + 4 - d) % 4, p.x, p.y, p.c)
        self.arrived(ref, d - 1)
        self.go(ref, ref, 3 + d, p.device(x=1 - p.x))
        self.go(ref, ref, 7 + d, p.device(y=1 - p.y))
        self.go(ref, ref, 19 + d, p.device(c=1 - p.c))

    def cross(self, d):
        p = self.p
        z = (p.z + 4 - d) % 4
        ref = self.at(z, 1 - p.x, p.y, p.c)
        self.arrived(ref, 3 + d)
        if self.half:
            part = self.at(z, 1 - p.x, p.y, p.c, 0)
            self.go(part, part, 11 + d, p.device(y=1 - p.y))
        self.go(ref, ref, 23 + d, p.device(c=1 - p.c))
        ref = self.at(z, p.x, 1 - p.y, p.c)
        self.arrived(ref, 7 + d)
        part = self.at(z, p.x, 1 - p.y, p.c, 1)
        self.go(part, part, 15 + d, p.device(x=1 - p.x))
        self.go(ref, ref, 27 + d, p.device(c=1 - p.c))

    def corner(self, d):
        p = self.p
        z = (p.z + 4 - d) % 4
        if self.half:
            self.arrived(self.at(z, 1 - p.x, 1 - p.y, p.c, 0), 11 + d)
        self.arrived(self.at(z, 1 - p.x, 1 - p.y, p.c, 1), 15 + d)
        ref = self.at(z, 1 - p.x, 1 - p.y, p.c)
        self.go(ref, ref, 31 + d, p.device(c=1 - p.c))

    def finish(self):
        p = self.p
        other = 1 - p.c
        for d in range(4):
            z = (p.z + 4 - d) % 4
            self.arrived(self.at(z, p.x, p.y, other), 19 + d)
            self.arrived(self.at(z, 1 - p.x, p.y, other), 23 + d)
            self.arrived(self.at(z, p.x, 1 - p.y, other), 27 + d)
            self.arrived(self.at(z, 1 - p.x, 1 - p.y, other), 31 + d)

    def drain(self):
        pltpu.make_async_copy(self.shard, self.at(0, 0, 0, 0), self.local_sem).wait()
        for slot in range(self.SLOTS):
            part = 0 if 11 <= slot < 15 else 1 if 15 <= slot < 19 else None
            if part == 0 and not self.half:
                continue
            ref = self.at(0, 0, 0, 0, part)
            pltpu.make_async_copy(ref, ref, self.send_sem.at[slot]).wait()


def gather_steps(jobs):
    stages = []
    for i, job in enumerate(jobs):
        line = [functools.partial(job.line, d) for d in (1, 2, 3)]
        cross = [functools.partial(job.cross, d) for d in range(4)]
        corner = [functools.partial(job.corner, d) for d in range(4)]
        stages += [((i, 0, k), f) for k, f in enumerate(line)]
        stages += [((i + 1, 1, k), f) for k, f in enumerate(cross)]
        stages += [((i + 2, 2, k), f) for k, f in enumerate(corner)]
    return [f for _, f in sorted(stages, key=lambda pair: pair[0])]


def gather_scratch(count):
    return [
        pltpu.SemaphoreType.DMA((count,)),
        pltpu.SemaphoreType.DMA((count, Gather.SLOTS)),
        pltpu.SemaphoreType.DMA((count, Gather.SLOTS)),
    ]


def whole_shape(shard):
    return jax.ShapeDtypeStruct((4, 2, 2, 2) + shard.shape, shard.dtype)


def gather_first_kernel(count, *refs):
    vectors, table, shard = refs[:count], refs[count], refs[count + 1]
    whole, whole_tile, tile, local_sem, send_sem, recv_sem = refs[count + 2 :]
    tile[...] = jnp.zeros_like(tile)
    for i, v in enumerate(vectors):
        tile[i : i + 1, : v.shape[1]] = v[...].astype(f32)
    tile[16:24, : table.shape[1]] = table[...].astype(f32)
    place = Place()
    place.greet()
    pairs = [(shard, whole), (tile, whole_tile)]
    jobs = [Gather(place, s, w, local_sem.at[i], send_sem.at[i], recv_sem.at[i]) for i, (s, w) in enumerate(pairs)]
    for job in jobs:
        job.begin()
    for step in gather_steps(jobs):
        step()
    for job in jobs:
        job.finish()
    for job in jobs:
        job.drain()


def gather_first(shard, vectors, table):
    tile = jax.ShapeDtypeStruct((24, 128), f32)
    whole, tiles = pl.pallas_call(
        functools.partial(gather_first_kernel, len(vectors)),
        in_specs=[pl.BlockSpec(memory_space=pltpu.VMEM)] * (len(vectors) + 2),
        out_specs=[pl.BlockSpec(memory_space=pl.ANY)] * 2,
        out_shape=[whole_shape(shard), whole_shape(tile)],
        scratch_shapes=[pltpu.VMEM((24, 128), f32)] + gather_scratch(2),
        compiler_params=pltpu.CompilerParams(collective_id=0, has_side_effects=True),
        name="gather_first",
    )(*[v[None, :] for v in vectors], table, shard)
    return whole.reshape(32 * shard.shape[0], shard.shape[1]), tiles.reshape(32, 24, 128)


class Reduce:
    SLOTS = 12

    @staticmethod
    def scratch(shape, dtype):
        rows, width = shape
        half = (width // 256) * 128
        four = lambda w: pltpu.VMEM((4, rows, w), dtype)
        return [
            pltpu.VMEM((4, 4, rows, width), dtype),
            pltpu.VMEM((4, 4, rows, width), dtype),
            four(max(half, 128)), four(width - half), four(width), four(width),
            pltpu.VMEM((3, rows, width), dtype),
            pltpu.SemaphoreType.DMA((Reduce.SLOTS,)),
            pltpu.SemaphoreType.DMA((Reduce.SLOTS,)),
        ]

    def __init__(self, place, parts, out, scratch):
        self.p, self.parts, self.out = place, parts, out
        (self.other, self.ready, self.by_y, self.by_x, self.from_x, self.from_y, self.from_z,
         self.send_sem, self.recv_sem) = scratch
        width = out.shape[-1]
        self.half, self.width = (width // 256) * 128, width

    def go(self, src, dst, slot, to):
        send(src, dst, self.send_sem.at[slot], self.recv_sem.at[slot], to)

    def arrived(self, dst, slot):
        pltpu.make_async_copy(dst, dst, self.recv_sem.at[slot]).wait()

    def spots(self):
        p = self.p
        return [(1 - p.x, 1 - p.y), (1 - p.x, p.y), (p.x, 1 - p.y), (p.x, p.y)]

    def begin(self):
        p = self.p
        for i, (x, y) in enumerate(self.spots()):
            self.go(self.parts.at[:, x, y, 1 - p.c], self.other.at[i], i, p.device(c=1 - p.c))

    def pair(self, i, z):
        x, y = self.spots()[i]
        return self.parts[z, x, y, self.p.c].astype(f32) + self.other[i, z].astype(f32)

    def corner(self):
        p, half = self.p, self.half
        self.arrived(self.other.at[0], 0)

        @pl.loop(0, 4)
        def _(z):
            self.ready[0, z] = self.pair(0, z).astype(self.ready.dtype)

        if half:
            self.go(self.ready.at[0, :, :, pl.ds(0, half)], self.by_y, 4, p.device(y=1 - p.y))
        self.go(self.ready.at[0, :, :, pl.ds(half, self.width - half)], self.by_x, 5, p.device(x=1 - p.x))

    def cross(self):
        p, half = self.p, self.half
        self.arrived(self.other.at[1], 1)
        if half:
            self.arrived(self.by_y, 4)

        @pl.loop(0, 4)
        def _(z):
            total = self.pair(1, z)
            if half:
                total = jnp.concatenate([total[:, :half] + self.by_y[z].astype(f32), total[:, half:]], axis=1)
            self.ready[1, z] = total.astype(self.ready.dtype)

        self.go(self.ready.at[1], self.from_x, 6, p.device(x=1 - p.x))

    def cross_y(self):
        p, half = self.p, self.half
        self.arrived(self.other.at[2], 2)
        self.arrived(self.by_x, 5)

        @pl.loop(0, 4)
        def _(z):
            total = self.pair(2, z)
            right = total[:, half:] + self.by_x[z].astype(f32)
            total = jnp.concatenate([total[:, :half], right], axis=1) if half else right
            self.ready[2, z] = total.astype(self.ready.dtype)

        self.go(self.ready.at[2], self.from_y, 7, p.device(y=1 - p.y))

    def line(self):
        p = self.p
        self.arrived(self.other.at[3], 3)
        self.arrived(self.from_x, 6)
        self.arrived(self.from_y, 7)
        for d in (1, 2, 3):
            z = (p.z + d) % 4
            total = self.pair(3, z) + self.from_x[z].astype(f32) + self.from_y[z].astype(f32)
            self.ready[3, z] = total.astype(self.ready.dtype)
            self.go(self.ready.at[3, z], self.from_z.at[d - 1], 7 + d, p.device(z=z))

    def finish(self):
        p = self.p
        for d in (1, 2, 3):
            self.arrived(self.from_z.at[d - 1], 7 + d)
        total = self.pair(3, p.z) + self.from_x[p.z].astype(f32) + self.from_y[p.z].astype(f32)
        for d in (1, 2, 3):
            total = total + self.from_z[d - 1].astype(f32)
        self.out[...] = total

    def drain(self):
        for slot in range(11):
            if slot == 4 and not self.half:
                continue
            ref = (self.by_y if slot == 4 else self.by_x if slot == 5 else
                   self.other.at[0] if slot < 8 else self.from_z.at[0])
            pltpu.make_async_copy(ref, ref, self.send_sem.at[slot]).wait()


class Everywhere:
    @staticmethod
    def scratch(shape):
        return [pltpu.VMEM((3,) + shape, f32), pltpu.VMEM((6,) + shape, f32),
                pltpu.SemaphoreType.DMA((6,)), pltpu.SemaphoreType.DMA((6,))]

    def __init__(self, place, block, out, scratch):
        self.p, self.block, self.out = place, block, out
        self.mine, self.got, self.send_sem, self.recv_sem = scratch

    def go(self, src, slot, to):
        send(src, self.got.at[slot], self.send_sem.at[slot], self.recv_sem.at[slot], to)

    def arrived(self, slot):
        dst = self.got.at[slot]
        pltpu.make_async_copy(dst, dst, self.recv_sem.at[slot]).wait()

    def begin(self):
        self.go(self.block, 0, self.p.device(c=1 - self.p.c))

    def corner(self):
        self.arrived(0)
        self.mine[0] = self.block[...] + self.got[0]
        self.go(self.mine.at[0], 1, self.p.device(x=1 - self.p.x))

    def cross(self):
        self.arrived(1)
        self.mine[1] = self.mine[0] + self.got[1]
        self.go(self.mine.at[1], 2, self.p.device(y=1 - self.p.y))

    def cross_y(self):
        pass

    def line(self):
        p = self.p
        self.arrived(2)
        self.mine[2] = self.mine[1] + self.got[2]
        for d in (1, 2, 3):
            self.go(self.mine.at[2], 2 + d, p.device(z=(p.z + d) % 4))

    def finish(self):
        p = self.p
        for d in (1, 2, 3):
            self.arrived(2 + d)
        total = None
        for z in range(4):
            term = jnp.where(p.z == z, self.mine[2], 0.0)
            for d in (1, 2, 3):
                term = term + jnp.where((p.z + 4 - d) % 4 == z, self.got[2 + d], 0.0)
            total = term if total is None else total + term
        self.out[...] = total

    def drain(self):
        for slot in range(6):
            ref = self.got.at[slot]
            pltpu.make_async_copy(ref, ref, self.send_sem.at[slot]).wait()


def reduce_steps(jobs):
    stages = []
    for i, job in enumerate(jobs):
        stages += [((i, 0), job.corner), ((i + 1, 1), job.cross), ((i + 1, 2), job.cross_y), ((i + 2, 3), job.line)]
    return [f for _, f in sorted(stages, key=lambda pair: pair[0])]


def reduce_kernel(count, extra, *refs):
    total = count + extra
    parts, outs, scratch = refs[:total], refs[total : 2 * total], refs[2 * total :]
    place = Place()
    place.greet()
    jobs = [Reduce(place, parts[i], outs[i], scratch[9 * i : 9 * i + 9]) for i in range(count)]
    if extra:
        jobs.append(Everywhere(place, parts[count], outs[count], scratch[9 * count :]))
    for job in jobs:
        job.begin()
    for step in reduce_steps(jobs):
        step()
    for job in jobs:
        job.finish()
    for job in jobs:
        job.drain()


def reduce_all(parts, block, collective_id):
    shapes = [(p.shape[0] // 32, p.shape[1]) for p in parts]
    given = [p.reshape((4, 2, 2, 2) + s) for p, s in zip(parts, shapes)]
    outs = [jax.ShapeDtypeStruct(s, f32) for s in shapes]
    scratch = []
    for p, s in zip(parts, shapes):
        scratch += Reduce.scratch(s, p.dtype)
    extra = block is not None
    if extra:
        given.append(block)
        outs.append(jax.ShapeDtypeStruct(block.shape, f32))
        scratch += Everywhere.scratch(block.shape)
    return pl.pallas_call(
        functools.partial(reduce_kernel, len(parts), int(extra)),
        in_specs=[pl.BlockSpec(memory_space=pltpu.VMEM)] * len(given),
        out_specs=[pl.BlockSpec(memory_space=pltpu.VMEM)] * len(outs),
        out_shape=outs,
        scratch_shapes=scratch,
        compiler_params=pltpu.CompilerParams(
            collective_id=collective_id, has_side_effects=True, vmem_limit_bytes=60 * 2**20
        ),
        name="reduce_all",
    )(*given)


def finish_kernel(count, sizes, *refs):
    tile, sums, outs = refs[0], refs[1 : 1 + count], refs[1 + count :]
    for src, dst in zip(sums, outs):
        dst[...] = src[...]
    for i, size in enumerate(sizes):
        outs[count + i][...] = tile[i : i + 1, :size]
    table = outs[count + len(sizes)]
    table[...] = tile[16:24, : table.shape[1]]


def finish(tile, sums, sizes, columns):
    outs = [jax.ShapeDtypeStruct(a.shape, f32) for a in sums]
    outs += [jax.ShapeDtypeStruct((1, n), f32) for n in sizes] + [jax.ShapeDtypeStruct((8, columns), f32)]
    out = pl.pallas_call(
        functools.partial(finish_kernel, len(sums), sizes),
        in_specs=[pl.BlockSpec(memory_space=pltpu.VMEM)] * (1 + len(sums)),
        out_specs=[pl.BlockSpec(memory_space=pltpu.VMEM)] * len(outs),
        out_shape=outs,
        name="finish",
    )(tile, *sums)
    n = len(sums)
    return out[:n], [v.reshape(-1) for v in out[n : n + len(sizes)]], out[-1]

AXES = ("wide", "narrow")


def standardize(v):
    centred = v - jnp.mean(v, axis=-1, keepdims=True)
    inverse = lax.rsqrt(jnp.mean(centred * centred, axis=-1, keepdims=True) + 1e-05)
    return centred * inverse, inverse


def norm_back(grad, normed, inverse, gain):
    scaled = grad * gain
    return inverse * (
        scaled
        - jnp.mean(scaled, axis=-1, keepdims=True)
        - normed * jnp.mean(scaled * normed, axis=-1, keepdims=True)
    )


def lanes(x):
    return jnp.pad(x, ((0, 0), (0, 0), (0, 128 - x.shape[2])))


def pack_tiles(vectors, table, devices):
    rows = [lanes(v.reshape(devices, 1, -1)) for v in vectors]
    rows.append(jnp.zeros((devices, 16 - len(vectors), 128), f32))
    rows.append(lanes(table.reshape(devices, 8, -1)))
    return jnp.concatenate(rows, axis=1)


def unpack_tiles(tiles, sizes, columns):
    vectors = [tiles[:, i, :size].reshape(-1) for i, size in enumerate(sizes)]
    return vectors, tiles[:, 16:24, :columns].reshape(-1, columns)


def whole_of(x):
    return lax.all_gather(x, AXES, axis=0, tiled=True)


def share_of(x):
    return lax.psum_scatter(x, AXES, scatter_dimension=0, tiled=True)


def local(devices, direct, tokens, cotangent, segments, buckets, norm1_gain, norm1_bias, qkv_weight, qv_bias,
          head_scale, rel_table, out_weight, out_bias, post_gain, post_bias, norm2_gain, norm2_bias,
          fc1_weight, fc1_bias, inner_gain, inner_bias, fc2_weight, fc2_bias):
    seq, width = tokens.shape
    heads = head_scale.shape[0]
    size = width // heads
    small = (norm1_gain, norm1_bias, out_bias, post_gain, post_bias, norm2_gain, norm2_bias, fc2_bias,
             qv_bias, fc1_bias, inner_gain, inner_bias)
    sizes = [v.shape[0] for v in small]
    nb = rel_table.shape[0] * devices
    held = bf16 if direct else f32
    late = (out_weight, fc1_weight, fc2_weight)
    if direct:
        w_qkv, tiles = gather_first(qkv_weight, small, rel_table)
        vectors, table = unpack_tiles(tiles, sizes, heads)
    else:
        w_qkv = whole_of(qkv_weight)
        vectors = [whole_of(v).astype(f32) for v in small]
        table = whole_of(rel_table).astype(f32)
        w_out, w_first, w_second = [whole_of(w) for w in late]
        late = ()
    (gain_one, bias_one, bias_out, gain_post, bias_post, gain_two, bias_two, bias_second,
     bias_qv, bias_first, gain_inner, bias_inner) = vectors
    table_t = table.T.reshape(heads // 2, 2, nb)
    scale = jnp.repeat(head_scale.astype(f32), size)[None, :]

    inputs = tokens.astype(f32)
    hat_one, inv_one = standardize(inputs)
    h_one = (hat_one * gain_one + bias_one).astype(bf16)
    shift = jnp.concatenate([bias_qv[:width], jnp.zeros((width,), f32), bias_qv[width:]])
    qkv = (dot(h_one, w_qkv) + shift).astype(bf16)
    attn, probs, wholes = attention_forward(qkv, table_t, buckets, segments, late)
    if direct:
        w_out, w_first, w_second = wholes
    scaled = (attn * scale).astype(bf16)
    mixed = dot(scaled, w_out) + bias_out
    hat_post, inv_post = standardize(mixed)
    first = inputs + hat_post * gain_post + bias_post
    hat_two, inv_two = standardize(first)
    h_two = (hat_two * gain_two + bias_two).astype(bf16)
    inner = dot(h_two, w_first) + bias_first
    cdf = 0.5 * (1.0 + lax.erf(inner * (1.0 / math.sqrt(2.0))))
    hat_inner, inv_inner = standardize(inner * cdf)
    hidden = (hat_inner * gain_inner + bias_inner).astype(bf16)
    output = (first + (dot(hidden, w_second) + bias_second)).astype(bf16)

    grad_out = cotangent.astype(f32)
    g_second = dot(hidden, cotangent, TN).astype(held)
    g_second_bias = jnp.sum(grad_out, axis=0)
    d_hidden = dot(cotangent, w_second, NT)
    g_inner_gain = jnp.sum(d_hidden * hat_inner, axis=0)
    g_inner_bias = jnp.sum(d_hidden, axis=0)
    d_gelu = norm_back(d_hidden, hat_inner, inv_inner, gain_inner)
    pdf = jnp.exp(-0.5 * inner * inner) * (1.0 / math.sqrt(2.0 * math.pi))
    d_inner = (d_gelu * (cdf + inner * pdf)).astype(bf16)
    g_first_bias = jnp.sum(d_inner.astype(f32), axis=0)
    g_first = dot(h_two, d_inner, TN).astype(held)
    d_two = dot(d_inner, w_first, NT)
    g_two_gain = jnp.sum(d_two * hat_two, axis=0)
    g_two_bias = jnp.sum(d_two, axis=0)
    d_first = grad_out + norm_back(d_two, hat_two, inv_two, gain_two)
    g_post_gain = jnp.sum(d_first * hat_post, axis=0)
    g_post_bias = jnp.sum(d_first, axis=0)
    d_mixed = norm_back(d_first, hat_post, inv_post, gain_post).astype(bf16)
    g_out_bias = jnp.sum(d_mixed.astype(f32), axis=0)
    g_out = dot(scaled, d_mixed, TN).astype(held)
    d_scaled = dot(d_mixed, w_out, NT)
    g_scale = jnp.sum(jnp.sum(d_scaled * attn, axis=0).reshape(heads, size), axis=1)
    d_attn = (d_scaled * scale).astype(bf16)
    early = (g_second, g_first, g_out)
    dq, dk, dv, hist, sums = attention_backward(
        qkv, d_attn, attn, probs, buckets, nb, early if direct else ())
    g_table = table_gradient(hist, heads)
    dqkv = jnp.concatenate([dq, dk, dv], axis=1)
    g_qv = jnp.concatenate([jnp.sum(dq.astype(f32), axis=0), jnp.sum(dv.astype(f32), axis=0)])
    g_qkv = dot(h_one, dqkv, TN).astype(held)
    d_one = dot(dqkv, w_qkv, NT)
    g_one_gain = jnp.sum(d_one * hat_one, axis=0)
    g_one_bias = jnp.sum(d_one, axis=0)
    grad_tokens = (d_first + norm_back(d_one, hat_one, inv_one, gain_one)).astype(bf16)

    grads = (g_one_gain, g_one_bias, g_out_bias, g_post_gain, g_post_bias, g_two_gain, g_two_bias,
             g_second_bias, g_qv, g_first_bias, g_inner_gain, g_inner_bias)
    if direct:
        block = jnp.pad(g_scale[None, :], ((0, 7), (0, 128 - heads)))
        tiles = pack_tiles(grads, g_table, devices).reshape(devices * 24, 128)
        g_qkv, tile, block = reduce_all([g_qkv, tiles], block, 1)
        g_scale = block[0, :heads]
        (g_second, g_first, g_out, g_qkv), grads, g_table = finish(tile, [*sums, g_qkv], sizes, heads)
    else:
        g_second, g_first, g_out, g_qkv = [share_of(g) for g in (*early, g_qkv)]
        grads = [share_of(g) for g in grads]
        g_table = share_of(g_table)
        g_scale = lax.psum(g_scale, AXES)
    (g_one_gain, g_one_bias, g_out_bias, g_post_gain, g_post_bias, g_two_gain, g_two_bias,
     g_second_bias, g_qv, g_first_bias, g_inner_gain, g_inner_bias) = grads
    return (output, grad_tokens, g_one_gain, g_one_bias, g_qkv, g_qv, g_scale, g_table, g_out, g_out_bias,
            g_post_gain, g_post_bias, g_two_gain, g_two_bias, g_first, g_first_bias, g_inner_gain,
            g_inner_bias, g_second, g_second_bias)


def solution(mesh):
    devices = mesh.shape["wide"] * mesh.shape["narrow"]
    direct = (mesh.shape["wide"], mesh.shape["narrow"]) == (8, 4)
    split, line, whole = P(AXES, None), P(AXES), P()
    return jax.shard_map(
        functools.partial(local, devices, direct),
        mesh=mesh,
        in_specs=(split, split, split, whole, line, line, split, line, whole, split, split, line, line,
                  line, line, line, split, line, line, line, split, line),
        out_specs=(split, split, line, line, split, line, whole, split, split, line, line, line, line,
                   line, split, line, line, line, split, line),
        check_vma=False,
    )
```

```python
import functools
import math

import jax, jax.numpy as jnp
from jax import lax
from jax.experimental import pallas as pl
from jax.experimental.pallas import tpu as pltpu
from jax.sharding import PartitionSpec as P

f32 = jnp.float32
bf16 = jnp.bfloat16
NT = (((1,), (1,)), ((), ()))
TN = (((0,), (0,)), ((), ()))


def dot(a, b, dims=(((1,), (0,)), ((), ()))):
    return lax.dot_general(a, b, dims, preferred_element_type=f32)


def lookup(row, index):
    shape = index.shape
    low = jnp.broadcast_to(row[:, :128], shape)
    high = jnp.broadcast_to(row[:, 128:], shape)
    inner = index & 127
    return jnp.where(
        index < 128,
        jnp.take_along_axis(low, inner, axis=1),
        jnp.take_along_axis(high, inner, axis=1),
    )


def forward_half(half, q_ref, k_ref, v_ref, table_ref, buckets_ref, segc_ref, segr_ref, attn_ref, p_ref):
    seq = q_ref.shape[0]
    even = lax.broadcasted_iota(jnp.int32, (1, 128), 1) < 64
    mine = even if half == 0 else jnp.logical_not(even)
    rows = 128
    row = table_ref[0, half : half + 1, :]
    k = k_ref[...]
    v = v_ref[...]

    def body(step, carry):
        at = pl.ds(pl.multiple_of(step * rows, rows), rows)
        q = jnp.where(mine, q_ref[at, :], jnp.zeros((), bf16))
        raw = dot(q, k, NT) * 0.125
        bias = jnp.concatenate(
            [lookup(row, buckets_ref[at, pl.ds(128 * j, 128)]) for j in range(seq // 128)], axis=1
        )
        same = segc_ref[at, :] == segr_ref[...]
        scores = jnp.where(same, raw + bias, -1e9)
        top = jnp.max(scores, axis=1, keepdims=True)
        expo = jnp.exp(scores - top)
        total = jnp.sum(expo, axis=1, keepdims=True)
        probs = (expo * (1.0 / total)).astype(bf16)
        p_ref[half, at, :] = probs
        out = dot(probs, v)
        if half == 0:
            attn_ref[at, :] = out
        else:
            attn_ref[at, :] = jnp.where(even, attn_ref[at, :], out)
        return carry

    lax.fori_loop(0, seq // rows, body, 0)


def forward_kernel(*refs):
    for half in range(2):
        forward_half(half, *refs)


def spread(steps, first, slots):
    plan = [[] for _ in range(slots)]
    plan[0] += first
    for i, step in enumerate(steps):
        plan[1 + i * (slots - 1) // len(steps)].append(step)
    return plan


def run_at(where, plan):
    for k, steps in enumerate(plan):
        if steps:

            @pl.when(where == k)
            def _():
                for step in steps:
                    step()


def flatten_row(tiles_ref, row, size):
    block = tiles_ref[pl.ds(row, 32, stride=24), :].astype(bf16)
    shape = (128, 32 * size)
    lane = lax.broadcasted_iota(jnp.int32, shape, 1)
    pick = jnp.where(lane % size == lax.broadcasted_iota(jnp.int32, shape, 0), 1.0, 0.0).astype(bf16)
    shape = (32, 32 * size)
    owner = lax.broadcasted_iota(jnp.int32, shape, 1) // size == lax.broadcasted_iota(jnp.int32, shape, 0)
    return jnp.sum(jnp.where(owner, dot(block, pick), 0.0), axis=0, keepdims=True)


def forward_all_kernel(count, pairs, *refs):
    vectors, table, shards = refs[:count], refs[count], refs[count + 1 : count + 5]
    tokens_ref, buckets_ref, segc_ref, segr_ref = refs[count + 5 : count + 9]
    attn_ref, p_ref, qkv_ref, h_ref, narrow_ref, wide_ref, *wholes = refs[count + 9 : count + 19]
    tile, tiles_ref, w_ref, rows_ref, tile_rows, w_sem, local_sem, send_sem, recv_sem = refs[count + 19 :]
    pair = pl.program_id(0)
    seq, width = tokens_ref.shape
    columns = table.shape[1]
    place = Place()
    jobs = [
        Gather(place, s, w, local_sem.at[i], send_sem.at[i], recv_sem.at[i])
        for i, (s, w) in enumerate(zip((shards[0], tile, *shards[1:]), (wholes[0], tiles_ref, *wholes[1:])))
    ]
    now, later = jobs[:2], jobs[2:]
    rest = gather_steps(later)
    plan = spread(rest[3:], [], 2 * pairs)

    @pl.when(pair == 0)
    def _():
        tile[...] = jnp.zeros_like(tile)
        for i, v in enumerate(vectors):
            tile[i : i + 1, : v.shape[1]] = v[...].astype(f32)
        tile[16:24, :columns] = table[...].astype(f32)
        place.greet()
        for job in now:
            job.begin()
        for d in (1, 2, 3):
            for job in now:
                job.line(d)
        later[0].begin()
        later[1].begin()
        for d in range(4):
            for job in now:
                job.cross(d)
        later[2].begin()
        for d in range(4):
            for job in now:
                job.corner(d)
        for step in rest[:3]:
            step()
        for job in now:
            job.finish()
        weight = pltpu.make_async_copy(wholes[0], w_ref, w_sem)
        weight.start()
        gain = flatten_row(tiles_ref, 0, width // 32)
        bias = flatten_row(tiles_ref, 1, width // 32)
        shift = flatten_row(tiles_ref, 8, width // 16)
        shift = jnp.concatenate([shift[:, :width], jnp.zeros((1, width), f32), shift[:, width:]], axis=1)
        rows_ref[0:1, :] = shift
        narrow_ref[0:1, :] = gain
        narrow_ref[1:2, :] = bias
        rows = 128

        @pl.loop(0, seq // rows)
        def _(step):
            at = pl.ds(pl.multiple_of(step * rows, rows), rows)
            v = tokens_ref[at, :].astype(f32)
            v = v - jnp.mean(v, axis=1, keepdims=True)
            v = v * lax.rsqrt(jnp.mean(v * v, axis=1, keepdims=True) + 1e-05)
            h_ref[at, :] = (v * gain + bias).astype(bf16)

        weight.wait()

        @pl.loop(0, 9)
        def _(i):
            at = pl.ds(pl.multiple_of(256 * i, 256), 256)
            qkv_ref[:, at] = (dot(h_ref[...], w_ref[:, at]) + rows_ref[0:1, at]).astype(bf16)

        spots = tiles_ref.shape[0] // 24
        blocks = [tiles_ref[pl.ds(24 * d + 16, 8), :] for d in range(spots)]
        flat = jnp.concatenate(blocks, axis=0).T
        for i in range(pairs):
            tile_rows[i] = flat[2 * i : 2 * i + 2, :]

    q_ref, k_ref, v_ref = [qkv_ref.at[:, pl.ds(pl.multiple_of(width * i + pair * 128, 128), 128)] for i in range(3)]
    for half in range(2):
        run_at(pair, plan[half::2])
        forward_half(half, q_ref, k_ref, v_ref, tile_rows.at[pl.ds(pair, 1)], buckets_ref, segc_ref, segr_ref,
                     attn_ref, p_ref)

    @pl.when(pair == 1)
    def _():
        for i in range(2, 8):
            narrow_ref[i : i + 1, :] = flatten_row(tiles_ref, i, width // 32)
        deep = wide_ref.shape[1]
        wide_ref[...] = jnp.zeros_like(wide_ref)
        for i in range(3):
            wide_ref[i : i + 1, :] = flatten_row(tiles_ref, 9 + i, deep // 32)

    @pl.when(pair == pairs - 1)
    def _():
        for job in later:
            job.finish()
        for job in jobs:
            job.drain()


def forward_all(vectors, table, shards, tokens, buckets, segments):
    seq, width = tokens.shape
    pairs = width // 128
    vmem = pl.BlockSpec(memory_space=pltpu.VMEM)
    attn, probs, qkv, h_one, narrow, wide, *wholes = pl.pallas_call(
        functools.partial(forward_all_kernel, len(vectors), pairs),
        grid=(pairs,),
        in_specs=[vmem] * (len(vectors) + 9),
        out_specs=[
            pl.BlockSpec((seq, 128), lambda i: (0, i)),
            pl.BlockSpec((2, seq, seq), lambda i: (i, 0, 0)),
            vmem, vmem, vmem, vmem,
        ]
        + [pl.BlockSpec(memory_space=pl.ANY)] * 4,
        out_shape=[
            jax.ShapeDtypeStruct((seq, width), f32),
            jax.ShapeDtypeStruct((2 * pairs, seq, seq), bf16),
            jax.ShapeDtypeStruct((seq, 3 * width), bf16),
            jax.ShapeDtypeStruct((seq, width), bf16),
            jax.ShapeDtypeStruct((8, width), f32),
            jax.ShapeDtypeStruct((8, shards[2].shape[1]), f32),
        ]
        + [whole_shape(x) for x in shards],
        scratch_shapes=[
            pltpu.VMEM((24, 128), f32),
            pltpu.VMEM((768, 128), f32),
            pltpu.VMEM((width, 3 * width), bf16),
            pltpu.VMEM((8, 3 * width), f32),
            pltpu.VMEM((pairs, 2, 256), f32),
            pltpu.SemaphoreType.DMA,
        ]
        + gather_scratch(5),
        compiler_params=pltpu.CompilerParams(collective_id=2, has_side_effects=True, vmem_limit_bytes=60 * 2**20),
        name="forward_all",
    )(*[v[None, :] for v in vectors], table, *shards, tokens, buckets, segments.reshape(seq, 1),
      segments.reshape(1, seq))
    return attn, probs, qkv, h_one, narrow, wide, wholes


def attention_forward(qkv, table_t, buckets, segments):
    seq, width = qkv.shape[0], qkv.shape[1] // 3
    pairs = width // 128
    nb = table_t.shape[2]
    return pl.pallas_call(
        forward_kernel,
        grid=(pairs,),
        in_specs=[
            pl.BlockSpec((seq, 128), lambda i: (0, i)),
            pl.BlockSpec((seq, 128), lambda i: (0, pairs + i)),
            pl.BlockSpec((seq, 128), lambda i: (0, 2 * pairs + i)),
            pl.BlockSpec((1, 2, nb), lambda i: (i, 0, 0)),
            pl.BlockSpec((seq, seq), lambda i: (0, 0)),
            pl.BlockSpec((seq, 1), lambda i: (0, 0)),
            pl.BlockSpec((1, seq), lambda i: (0, 0)),
        ],
        out_specs=[
            pl.BlockSpec((seq, 128), lambda i: (0, i)),
            pl.BlockSpec((2, seq, seq), lambda i: (i, 0, 0)),
        ],
        out_shape=[
            jax.ShapeDtypeStruct((seq, width), f32),
            jax.ShapeDtypeStruct((2 * pairs, seq, seq), bf16),
        ],
        name="attention_forward",
    )(qkv, qkv, qkv, table_t, buckets, segments.reshape(seq, 1), segments.reshape(1, seq))


HIGH = 4


def backward_half(half, pair, q_ref, k_ref, v_ref, do_ref, attn_ref, p_ref, dq_ref, dk_ref, dv_ref, ds_ref, dst_ref):
    seq = q_ref.shape[0]
    even = lax.broadcasted_iota(jnp.int32, (1, 128), 1) < 64
    mine = even if half == 0 else jnp.logical_not(even)
    rows = 128
    chunks = seq // 128
    k = k_ref[...]
    v = v_ref[...]
    head = pair * 2 + half

    def body(step, carry):
        at = pl.ds(pl.multiple_of(step * rows, rows), rows)
        do = jnp.where(mine, do_ref[at, :], jnp.zeros((), bf16))
        probs = p_ref[half, at, :]
        delta = jnp.sum(do.astype(f32) * attn_ref[at, :], axis=1, keepdims=True)
        ds = probs.astype(f32) * (dot(do, v, NT) - delta)
        for j in range(chunks):
            ds_ref[j, pl.ds(step * rows * 16 + head, rows, stride=16), :] = ds[:, 128 * j : 128 * j + 128]
        ds = ds.astype(bf16)
        dst_ref[at, :] = ds
        dq = dot(ds, k) * 0.125
        if half == 0:
            dq_ref[at, :] = dq.astype(bf16)
        else:
            dq_ref[at, :] = jnp.where(even, dq_ref[at, :], dq.astype(bf16))
        return carry

    lax.fori_loop(0, seq // rows, body, 0)
    dk = (dot(dst_ref[...], q_ref[...], TN) * 0.125).astype(bf16)
    dv = dot(p_ref[half], do_ref[...], TN).astype(bf16)
    if half == 0:
        dk_ref[...] = dk
        dv_ref[...] = dv
    else:
        dk_ref[...] = jnp.where(even, dk_ref[...], dk)
        dv_ref[...] = jnp.where(even, dv_ref[...], dv)


def histogram(part, parts, buckets_ref, ds_ref, acc_ref):
    seq = buckets_ref.shape[0]
    chunks = seq // 128
    group = 8
    low = acc_ref.shape[1]

    def body(step, carry):
        base = pl.multiple_of(step * group, group)
        ids = buckets_ref[pl.ds(base, group), :]
        left, right = [], []
        for r in range(group):
            at = pl.ds(pl.multiple_of((base + r) * 16, 16), 16)
            d = jnp.concatenate([ds_ref[j, at, :] for j in range(chunks)], axis=1)
            idr = ids[r : r + 1, :]
            top = idr // low
            left.append(jnp.concatenate([jnp.where(top == b, d, 0.0) for b in range(HIGH)], axis=0).astype(bf16))
            which = lax.broadcasted_iota(jnp.int32, (low, seq), 0)
            right.append(jnp.where(which == (idr & (low - 1)), 1.0, 0.0).astype(bf16))
        acc_ref[...] += dot(jnp.concatenate(left, axis=1), jnp.concatenate(right, axis=1), NT)
        return carry

    steps = seq // group // parts
    lax.fori_loop(part * steps, (part + 1) * steps, body, 0)


def backward_kernel(*refs):
    ins, buckets_ref, outs, hist_ref = refs[:6], refs[6], refs[7:10], refs[10]
    ds_ref, dst_ref, acc_ref = refs[11:]
    pair = pl.program_id(0)
    for half in range(2):
        backward_half(half, pair, *ins, *outs, ds_ref, dst_ref)

    @pl.when(pair == pl.num_programs(0) - 1)
    def _():
        acc_ref[...] = jnp.zeros_like(acc_ref)
        histogram(0, 1, buckets_ref, ds_ref, acc_ref)
        hist_ref[...] = acc_ref[...]


def attention_backward(qkv, d_attn, attn, p, buckets, nb):
    seq, width = d_attn.shape
    pairs = width // 128
    low = nb // HIGH
    narrow = lambda first: pl.BlockSpec((seq, 128), lambda i: (0, first + i))
    return pl.pallas_call(
        backward_kernel,
        grid=(pairs,),
        in_specs=[
            narrow(0), narrow(pairs), narrow(2 * pairs), narrow(0), narrow(0),
            pl.BlockSpec((2, seq, seq), lambda i: (i, 0, 0)),
            pl.BlockSpec((seq, seq), lambda i: (0, 0)),
        ],
        out_specs=[narrow(0), narrow(0), narrow(0), pl.BlockSpec((HIGH * 16, low), lambda i: (0, 0))],
        out_shape=[jax.ShapeDtypeStruct((seq, width), bf16)] * 3
        + [jax.ShapeDtypeStruct((HIGH * 16, low), f32)],
        scratch_shapes=backward_scratch(seq, low),
        name="attention_backward",
    )(qkv, qkv, qkv, d_attn, attn, p, buckets)


def backward_scratch(seq, low):
    return [
        pltpu.VMEM((seq // 128, seq * 16, 128), f32),
        pltpu.VMEM((seq, seq), bf16),
        pltpu.VMEM((HIGH * 16, low), f32),
    ]


PARTS = 4


def owners(row, size):
    n = 32 * size
    lane = lax.broadcasted_iota(jnp.int32, (128, n), 1)
    pick = jnp.where(lane % size == lax.broadcasted_iota(jnp.int32, (128, n), 0), 1.0, 0.0)
    owner = lax.broadcasted_iota(jnp.int32, (32, n), 1) // size == lax.broadcasted_iota(jnp.int32, (32, n), 0)
    return lax.dot_general(jnp.where(owner, row, 0.0), pick, NT, precision=lax.Precision.HIGHEST,
                           preferred_element_type=f32)


def place_of(d):
    return d // 8, d // 4 % 2, d // 2 % 2, d % 2


def backward_all_kernel(pairs, heads, *refs):
    ins, buckets_ref, tokens_ref, h_ref, first_ref, gain_ref, w_hbm = refs[:6], *refs[6:12]
    parts, narrow_ref, wide_ref = refs[12:15], refs[15], refs[16]
    grad_ref, sums, tile_out, block_out = refs[17], refs[18:22], refs[22], refs[23]
    ds_ref, dst_ref, acc_ref, dqkv_ref, w_ref, part_ref, flat_ref, tiles_ref, block, w_sem, *scratch = refs[24:]
    pair = pl.program_id(0)
    seq, width = tokens_ref.shape
    place = Place()
    job = lambda i, x, out: Reduce(place, x, out, scratch[8 * i : 8 * i + 8])
    early = [job(i, parts[i], sums[i]) for i in range(3)]
    weight, small = job(3, part_ref, sums[3]), job(4, tiles_ref, tile_out)
    early.append(Everywhere(place, block, block_out, scratch[40:]))
    fetch = pltpu.make_async_copy(w_hbm, w_ref, w_sem)
    plan = spread(reduce_steps(early), [place.greet] + [j.begin for j in early] + [fetch.start], 2 * pairs + PARTS)

    @pl.when(pair == 0)
    def _():
        head = lax.broadcasted_iota(jnp.int32, (128, width), 1) // (width // heads)
        pick = jnp.where(head == lax.broadcasted_iota(jnp.int32, (128, width), 0), 1.0, 0.0)
        block[...] = jnp.zeros_like(block)
        block[0:1, :] = lax.dot_general(narrow_ref[0:1, :], pick, NT, precision=lax.Precision.HIGHEST,
                                        preferred_element_type=f32)
        flat_ref[...] = jnp.zeros_like(flat_ref)

    @pl.when(pair == 1)
    def _():
        for i in range(2, 8):
            flat_ref[pl.ds(i, 32, stride=24), :] = owners(narrow_ref[i : i + 1, :], width // 32)
        for i in range(3):
            flat_ref[pl.ds(9 + i, 32, stride=24), :] = owners(wide_ref[i : i + 1, :], wide_ref.shape[1] // 32)

    dq_ref, dk_ref, dv_ref = [
        dqkv_ref.at[:, pl.ds(pl.multiple_of(width * i + pair * 128, 128), 128)] for i in range(3)
    ]
    for half in range(2):
        run_at(pair, plan[half : 2 * pairs : 2])
        backward_half(half, pair, *ins, dq_ref, dk_ref, dv_ref, ds_ref, dst_ref)

    @pl.when(pair == pairs - 1)
    def _():
        third = width // 2
        rows = part_ref.shape[4]
        each = third // rows

        @pl.loop(0, 3 * width // 256)
        def _(i):
            at = pl.ds(pl.multiple_of(256 * i, 256), 256)
            for j in range(2):
                block = dot(h_ref[:, third * j : third * j + third], dqkv_ref[:, at], TN).astype(bf16)
                for k in range(each):
                    z, x, y, c = place_of(each * j + k)
                    part_ref[z, x, y, c, :, at] = block[rows * k : rows * k + rows, :]

        weight.begin()
        acc_ref[...] = jnp.zeros_like(acc_ref)
        for part in range(PARTS):
            for step in plan[2 * pairs + part]:
                step()
            if part == 1:
                weight.corner()
            histogram(part, PARTS, buckets_ref, ds_ref, acc_ref)
        weight.cross()
        weight.cross_y()
        fetch.wait()
        gain_sum, bias_sum = jnp.zeros((1, width), f32), jnp.zeros((1, width), f32)
        size = 256
        for i in range(seq // size):
            at = pl.ds(size * i, size)
            d_one = dot(dqkv_ref[at, :], w_ref[...], NT)
            v = tokens_ref[at, :].astype(f32)
            v = v - jnp.mean(v, axis=1, keepdims=True)
            inverse = lax.rsqrt(jnp.mean(v * v, axis=1, keepdims=True) + 1e-05)
            hat = v * inverse
            gain_sum += jnp.sum(d_one * hat, axis=0, keepdims=True)
            bias_sum += jnp.sum(d_one, axis=0, keepdims=True)
            scaled = d_one * gain_ref[...]
            back = inverse * (scaled - jnp.mean(scaled, axis=1, keepdims=True)
                              - hat * jnp.mean(scaled * hat, axis=1, keepdims=True))
            grad_ref[at, :] = (first_ref[at, :] + back).astype(bf16)
        total = lambda first: jnp.sum(dqkv_ref[:, first : first + width].astype(f32), axis=0, keepdims=True)
        qv_sum = jnp.concatenate([total(0), total(2 * width)], axis=1)
        for row, value in ((0, gain_sum), (1, bias_sum), (8, qv_sum)):
            flat_ref[pl.ds(row, 32, stride=24), :] = owners(value, value.shape[1] // 32)
        table = acc_ref[...].T
        for d in range(32):
            flat_ref[24 * d + 16 : 24 * d + 24, 0:heads] = table[
                8 * (d % 8) : 8 * (d % 8) + 8, 16 * (d // 8) : 16 * (d // 8) + heads]

        @pl.loop(0, 32)
        def _(d):
            z, x, y, c = place_of(d)
            tiles_ref[z, x, y, c] = flat_ref[pl.ds(pl.multiple_of(24 * d, 8), 24), :]

        small.begin()
        weight.line()
        small.corner()
        small.cross()
        small.cross_y()
        small.line()
        jobs = [*early, weight, small]
        for j in jobs:
            j.finish()
        for j in jobs:
            j.drain()


def backward_all(qkv, d_attn, attn, p, buckets, tokens, h_one, d_first, gain, w_qkv, parts, narrow_sums, wide_sums, heads):
    seq, width = d_attn.shape
    pairs = width // 128
    low = 256 // HIGH
    narrow = lambda first: pl.BlockSpec((seq, 128), lambda i: (0, first + i))
    vmem = pl.BlockSpec(memory_space=pltpu.VMEM)
    shapes = [(x.shape[0] // 32, x.shape[1]) for x in parts]
    qkv_shape = (width // 32, 3 * width)
    scratch = []
    for shape in (*shapes, qkv_shape):
        scratch += Reduce.scratch(shape, bf16)
    scratch += Reduce.scratch((24, 128), f32)
    scratch += Everywhere.scratch((8, 128))
    given = [x.reshape((4, 2, 2, 2) + shape) for x, shape in zip(parts, shapes)]
    return pl.pallas_call(
        functools.partial(backward_all_kernel, pairs, heads),
        grid=(pairs,),
        in_specs=[
            narrow(0), narrow(pairs), narrow(2 * pairs), narrow(0), narrow(0),
            pl.BlockSpec((2, seq, seq), lambda i: (i, 0, 0)),
            vmem, vmem, vmem, vmem, vmem,
            pl.BlockSpec(memory_space=pl.ANY),
        ]
        + [vmem] * 5,
        out_specs=[vmem] * 7,
        out_shape=[jax.ShapeDtypeStruct((seq, width), bf16)]
        + [jax.ShapeDtypeStruct(shape, f32) for shape in (*shapes, qkv_shape)]
        + [jax.ShapeDtypeStruct((24, 128), f32), jax.ShapeDtypeStruct((8, 128), f32)],
        scratch_shapes=backward_scratch(seq, low)
        + [
            pltpu.VMEM((seq, 3 * width), bf16),
            pltpu.VMEM((width, 3 * width), bf16),
            pltpu.VMEM((4, 2, 2, 2) + qkv_shape, bf16),
            pltpu.VMEM((768, 128), f32),
            pltpu.VMEM((4, 2, 2, 2, 24, 128), f32),
            pltpu.VMEM((8, 128), f32),
            pltpu.SemaphoreType.DMA,
        ]
        + scratch,
        compiler_params=pltpu.CompilerParams(
            collective_id=3, has_side_effects=True, vmem_limit_bytes=67043328
        ),
        name="backward_all",
    )(qkv, qkv, qkv, d_attn, attn, p, buckets, tokens, h_one, d_first, gain, w_qkv, *given,
      narrow_sums, wide_sums)


def table_gradient(hist, heads):
    high, low = HIGH, hist.shape[1]
    return hist.reshape(high, 16, low)[:, :heads].transpose(0, 2, 1).reshape(high * low, heads)

MESH = pl.DeviceIdType.MESH


class Place:
    def __init__(self):
        wide, narrow = lax.axis_index("wide"), lax.axis_index("narrow")
        self.z, self.x = wide // 2, wide % 2
        self.y, self.c = narrow // 2, narrow % 2

    def device(self, z=None, x=None, y=None, c=None):
        z = self.z if z is None else z
        x = self.x if x is None else x
        y = self.y if y is None else y
        c = self.c if c is None else c
        return (z * 2 + x, y * 2 + c)

    def peers(self):
        out = [self.device(z=(self.z + d) % 4) for d in (1, 2, 3)]
        return out + [self.device(x=1 - self.x), self.device(y=1 - self.y), self.device(c=1 - self.c)]

    def greet(self):
        barrier = pltpu.get_barrier_semaphore()
        for peer in self.peers():
            pl.semaphore_signal(barrier, inc=1, device_id=peer, device_id_type=MESH)
        pl.semaphore_wait(barrier, 6)


def send(src, dst, send_sem, recv_sem, to):
    copy = pltpu.make_async_remote_copy(
        src_ref=src, dst_ref=dst, send_sem=send_sem, recv_sem=recv_sem, device_id=to, device_id_type=MESH
    )
    copy.start()
    return copy


class Gather:
    SLOTS = 35

    def __init__(self, place, shard, whole, local_sem, send_sem, recv_sem):
        self.p, self.shard, self.whole = place, shard, whole
        self.local_sem, self.send_sem, self.recv_sem = local_sem, send_sem, recv_sem
        self.width = shard.shape[-1]
        self.half = (self.width // 256) * 128

    def at(self, z, x, y, c, part=None):
        rows = self.shard.shape[0]
        at = pl.ds(pl.multiple_of((((z * 2 + x) * 2 + y) * 2 + c) * rows, rows), rows)
        if part == 0:
            return self.whole.at[at, pl.ds(0, self.half)]
        if part == 1:
            return self.whole.at[at, pl.ds(self.half, self.width - self.half)]
        return self.whole.at[at, :]

    def go(self, src, dst, slot, to):
        send(src, dst, self.send_sem.at[slot], self.recv_sem.at[slot], to)

    def arrived(self, dst, slot):
        pltpu.make_async_copy(dst, dst, self.recv_sem.at[slot]).wait()

    def begin(self):
        p = self.p
        mine = self.at(p.z, p.x, p.y, p.c)
        pltpu.make_async_copy(self.shard, mine, self.local_sem).start()
        for d in (1, 2, 3):
            self.go(self.shard, mine, d - 1, p.device(z=(p.z + d) % 4))
        self.go(self.shard, mine, 3, p.device(x=1 - p.x))
        self.go(self.shard, mine, 7, p.device(y=1 - p.y))
        self.go(self.shard, mine, 19, p.device(c=1 - p.c))

    def line(self, d):
        p = self.p
        ref = self.at((p.z + 4 - d) % 4, p.x, p.y, p.c)
        self.arrived(ref, d - 1)
        self.go(ref, ref, 3 + d, p.device(x=1 - p.x))
        self.go(ref, ref, 7 + d, p.device(y=1 - p.y))
        self.go(ref, ref, 19 + d, p.device(c=1 - p.c))

    def cross(self, d):
        p = self.p
        z = (p.z + 4 - d) % 4
        ref = self.at(z, 1 - p.x, p.y, p.c)
        self.arrived(ref, 3 + d)
        if self.half:
            part = self.at(z, 1 - p.x, p.y, p.c, 0)
            self.go(part, part, 11 + d, p.device(y=1 - p.y))
        self.go(ref, ref, 23 + d, p.device(c=1 - p.c))
        ref = self.at(z, p.x, 1 - p.y, p.c)
        self.arrived(ref, 7 + d)
        part = self.at(z, p.x, 1 - p.y, p.c, 1)
        self.go(part, part, 15 + d, p.device(x=1 - p.x))
        self.go(ref, ref, 27 + d, p.device(c=1 - p.c))

    def corner(self, d):
        p = self.p
        z = (p.z + 4 - d) % 4
        if self.half:
            self.arrived(self.at(z, 1 - p.x, 1 - p.y, p.c, 0), 11 + d)
        self.arrived(self.at(z, 1 - p.x, 1 - p.y, p.c, 1), 15 + d)
        ref = self.at(z, 1 - p.x, 1 - p.y, p.c)
        self.go(ref, ref, 31 + d, p.device(c=1 - p.c))

    def finish(self):
        p = self.p
        other = 1 - p.c
        pltpu.make_async_copy(self.shard, self.at(p.z, p.x, p.y, p.c), self.local_sem).wait()
        for d in range(4):
            z = (p.z + 4 - d) % 4
            self.arrived(self.at(z, p.x, p.y, other), 19 + d)
            self.arrived(self.at(z, 1 - p.x, p.y, other), 23 + d)
            self.arrived(self.at(z, p.x, 1 - p.y, other), 27 + d)
            self.arrived(self.at(z, 1 - p.x, 1 - p.y, other), 31 + d)

    def drain(self):
        for slot in range(self.SLOTS):
            part = 0 if 11 <= slot < 15 else 1 if 15 <= slot < 19 else None
            if part == 0 and not self.half:
                continue
            ref = self.at(0, 0, 0, 0, part)
            pltpu.make_async_copy(ref, ref, self.send_sem.at[slot]).wait()


def gather_steps(jobs):
    stages = []
    for i, job in enumerate(jobs):
        line = [functools.partial(job.line, d) for d in (1, 2, 3)]
        cross = [functools.partial(job.cross, d) for d in range(4)]
        corner = [functools.partial(job.corner, d) for d in range(4)]
        stages += [((i, 0, k), f) for k, f in enumerate(line)]
        stages += [((i + 1, 1, k), f) for k, f in enumerate(cross)]
        stages += [((i + 2, 2, k), f) for k, f in enumerate(corner)]
    return [f for _, f in sorted(stages, key=lambda pair: pair[0])]


def gather_scratch(count):
    return [
        pltpu.SemaphoreType.DMA((count,)),
        pltpu.SemaphoreType.DMA((count, Gather.SLOTS)),
        pltpu.SemaphoreType.DMA((count, Gather.SLOTS)),
    ]


def whole_shape(shard):
    return jax.ShapeDtypeStruct((32 * shard.shape[0], shard.shape[1]), shard.dtype)


class Reduce:
    SLOTS = 12

    @staticmethod
    def scratch(shape, dtype):
        rows, width = shape
        half = (width // 256) * 128
        four = lambda w: pltpu.VMEM((4, rows, w), dtype)
        return [
            pltpu.VMEM((4, 4, rows, width), dtype),
            four(max(half, 128)), four(width - half), four(width), four(width),
            pltpu.VMEM((3, rows, width), dtype),
            pltpu.SemaphoreType.DMA((Reduce.SLOTS,)),
            pltpu.SemaphoreType.DMA((Reduce.SLOTS,)),
        ]

    def __init__(self, place, parts, out, scratch):
        self.p, self.parts, self.out = place, parts, out
        (self.other, self.by_y, self.by_x, self.from_x, self.from_y, self.from_z,
         self.send_sem, self.recv_sem) = scratch
        width = out.shape[-1]
        self.half, self.width = (width // 256) * 128, width

    def go(self, src, dst, slot, to):
        send(src, dst, self.send_sem.at[slot], self.recv_sem.at[slot], to)

    def arrived(self, dst, slot):
        pltpu.make_async_copy(dst, dst, self.recv_sem.at[slot]).wait()

    def spots(self):
        p = self.p
        return [(1 - p.x, 1 - p.y), (1 - p.x, p.y), (p.x, 1 - p.y), (p.x, p.y)]

    def begin(self):
        p = self.p
        for i, (x, y) in enumerate(self.spots()):
            self.go(self.parts.at[:, x, y, 1 - p.c], self.other.at[i], i, p.device(c=1 - p.c))

    def pair(self, i, z):
        x, y = self.spots()[i]
        return self.parts[z, x, y, self.p.c].astype(f32) + self.other[i, z].astype(f32)

    def corner(self):
        p, half = self.p, self.half
        self.arrived(self.other.at[0], 0)

        @pl.loop(0, 4)
        def _(z):
            self.other[0, z] = self.pair(0, z).astype(self.other.dtype)

        if half:
            self.go(self.other.at[0, :, :, pl.ds(0, half)], self.by_y, 4, p.device(y=1 - p.y))
        self.go(self.other.at[0, :, :, pl.ds(half, self.width - half)], self.by_x, 5, p.device(x=1 - p.x))

    def cross(self):
        p, half = self.p, self.half
        self.arrived(self.other.at[1], 1)
        if half:
            self.arrived(self.by_y, 4)

        @pl.loop(0, 4)
        def _(z):
            total = self.pair(1, z)
            if half:
                total = jnp.concatenate([total[:, :half] + self.by_y[z].astype(f32), total[:, half:]], axis=1)
            self.other[1, z] = total.astype(self.other.dtype)

        self.go(self.other.at[1], self.from_x, 6, p.device(x=1 - p.x))

    def cross_y(self):
        p, half = self.p, self.half
        self.arrived(self.other.at[2], 2)
        self.arrived(self.by_x, 5)

        @pl.loop(0, 4)
        def _(z):
            total = self.pair(2, z)
            right = total[:, half:] + self.by_x[z].astype(f32)
            total = jnp.concatenate([total[:, :half], right], axis=1) if half else right
            self.other[2, z] = total.astype(self.other.dtype)

        self.go(self.other.at[2], self.from_y, 7, p.device(y=1 - p.y))

    def line(self):
        p = self.p
        self.arrived(self.other.at[3], 3)
        self.arrived(self.from_x, 6)
        self.arrived(self.from_y, 7)
        for d in (1, 2, 3):
            z = (p.z + d) % 4
            total = self.pair(3, z) + self.from_x[z].astype(f32) + self.from_y[z].astype(f32)
            self.other[3, z] = total.astype(self.other.dtype)
            self.go(self.other.at[3, z], self.from_z.at[d - 1], 7 + d, p.device(z=z))

    def finish(self):
        p = self.p
        for d in (1, 2, 3):
            self.arrived(self.from_z.at[d - 1], 7 + d)
        total = self.pair(3, p.z) + self.from_x[p.z].astype(f32) + self.from_y[p.z].astype(f32)
        for d in (1, 2, 3):
            total = total + self.from_z[d - 1].astype(f32)
        self.out[...] = total

    def drain(self):
        for slot in range(11):
            if slot == 4 and not self.half:
                continue
            ref = (self.by_y if slot == 4 else self.by_x if slot == 5 else
                   self.other.at[0] if slot < 8 else self.from_z.at[0])
            pltpu.make_async_copy(ref, ref, self.send_sem.at[slot]).wait()


class Everywhere:
    @staticmethod
    def scratch(shape):
        return [pltpu.VMEM((3,) + shape, f32), pltpu.VMEM((6,) + shape, f32),
                pltpu.SemaphoreType.DMA((6,)), pltpu.SemaphoreType.DMA((6,))]

    def __init__(self, place, block, out, scratch):
        self.p, self.block, self.out = place, block, out
        self.mine, self.got, self.send_sem, self.recv_sem = scratch

    def go(self, src, slot, to):
        send(src, self.got.at[slot], self.send_sem.at[slot], self.recv_sem.at[slot], to)

    def arrived(self, slot):
        dst = self.got.at[slot]
        pltpu.make_async_copy(dst, dst, self.recv_sem.at[slot]).wait()

    def begin(self):
        self.go(self.block, 0, self.p.device(c=1 - self.p.c))

    def corner(self):
        self.arrived(0)
        self.mine[0] = self.block[...] + self.got[0]
        self.go(self.mine.at[0], 1, self.p.device(x=1 - self.p.x))

    def cross(self):
        self.arrived(1)
        self.mine[1] = self.mine[0] + self.got[1]
        self.go(self.mine.at[1], 2, self.p.device(y=1 - self.p.y))

    def cross_y(self):
        pass

    def line(self):
        p = self.p
        self.arrived(2)
        self.mine[2] = self.mine[1] + self.got[2]
        for d in (1, 2, 3):
            self.go(self.mine.at[2], 2 + d, p.device(z=(p.z + d) % 4))

    def finish(self):
        p = self.p
        for d in (1, 2, 3):
            self.arrived(2 + d)
        total = None
        for z in range(4):
            term = jnp.where(p.z == z, self.mine[2], 0.0)
            for d in (1, 2, 3):
                term = term + jnp.where((p.z + 4 - d) % 4 == z, self.got[2 + d], 0.0)
            total = term if total is None else total + term
        self.out[...] = total

    def drain(self):
        for slot in range(6):
            ref = self.got.at[slot]
            pltpu.make_async_copy(ref, ref, self.send_sem.at[slot]).wait()


def reduce_steps(jobs):
    stages = []
    for i, job in enumerate(jobs):
        stages += [((i, 0), job.corner), ((i + 1, 1), job.cross), ((i + 1, 2), job.cross_y), ((i + 2, 3), job.line)]
    return [f for _, f in sorted(stages, key=lambda pair: pair[0])]


def finish_kernel(count, sizes, *refs):
    tile, block, sums, outs = refs[0], refs[1], refs[2 : 2 + count], refs[2 + count :]
    for src, dst in zip(sums, outs):
        dst[...] = src[...]
    for i, size in enumerate(sizes):
        outs[count + i][...] = tile[i : i + 1, :size]
    table, line = outs[count + len(sizes) :]
    table[...] = tile[16:24, : table.shape[1]]
    line[...] = block[0:1, : line.shape[1]]


def finish(tile, block, sums, sizes, columns):
    outs = [jax.ShapeDtypeStruct(a.shape, a.dtype) for a in sums]
    outs += [jax.ShapeDtypeStruct((1, n), f32) for n in sizes]
    outs += [jax.ShapeDtypeStruct((8, columns), f32), jax.ShapeDtypeStruct((1, columns), f32)]
    out = pl.pallas_call(
        functools.partial(finish_kernel, len(sums), sizes),
        in_specs=[pl.BlockSpec(memory_space=pltpu.VMEM)] * (2 + len(sums)),
        out_specs=[pl.BlockSpec(memory_space=pltpu.VMEM)] * len(outs),
        out_shape=outs,
        name="finish",
    )(tile, block, *sums)
    n = len(sums)
    return out[:n], [v.reshape(-1) for v in out[n : n + len(sizes)]], out[-2], out[-1].reshape(-1)

def row_norm(v):
    v = v - jnp.mean(v, axis=1, keepdims=True)
    inverse = lax.rsqrt(jnp.mean(v * v, axis=1, keepdims=True) + 1e-05)
    return v * inverse, inverse


def row_back(grad, hat, inverse, gain):
    scaled = grad * gain
    return inverse * (scaled - jnp.mean(scaled, axis=1, keepdims=True)
                      - hat * jnp.mean(scaled * hat, axis=1, keepdims=True))


def folded(v):
    total = v[:8]
    for i in range(1, v.shape[0] // 8):
        total = total + v[8 * i : 8 * i + 8]
    return total


def middle_kernel(attn_ref, tokens_ref, cot_ref, scale_ref, narrow_ref, wide_ref, w_out_hbm, w_first_hbm, w_second_hbm,
                  output_ref, d_first_ref, d_attn_ref, g_out_hbm, g_first_hbm, g_second_hbm, narrow_out, wide_out,
                  w_out, w_first, w_second, scaled, hat_post, stats, first, hat_two, h_two, h_two_t, inner, hat_inner,
                  hidden, d_hidden, d_mixed, g_out, g_first, g_second, acc_n, acc_w, in_sem, out_sem):
    seq, width = tokens_ref.shape
    deep = w_first.shape[1]
    fetches = [pltpu.make_async_copy(src, dst, in_sem.at[i]) for i, (src, dst) in enumerate(
        ((w_out_hbm, w_out), (w_first_hbm, w_first), (w_second_hbm, w_second)))]
    for fetch in fetches:
        fetch.start()
    narrow = lambda i: narrow_ref[i : i + 1, :]
    wide = lambda i: wide_ref[i : i + 1, :]
    acc_n[...] = jnp.zeros_like(acc_n)
    acc_w[...] = jnp.zeros_like(acc_w)
    half, group, chunk = 128, 16, 256

    def cols(i, size=chunk):
        return pl.ds(pl.multiple_of(i * size, size), size)

    fetches[0].wait()

    @pl.loop(0, seq // half)
    def _(i):
        at = cols(i, half)
        u = (attn_ref[at, :] * scale_ref[...]).astype(bf16)
        scaled[at, :] = u
        hat, inverse = row_norm(dot(u, w_out[...]) + narrow(2))
        hat_post[at, :] = hat
        stats[at, 0:1] = inverse
        x1 = tokens_ref[at, :].astype(f32) + hat * narrow(3) + narrow(4)
        first[at, :] = x1
        hat, inverse = row_norm(x1)
        hat_two[at, :] = hat
        stats[at, 1:2] = inverse
        h_two[at, :] = (hat * narrow(5) + narrow(6)).astype(bf16)

    fetches[1].wait()

    @pl.loop(0, deep // chunk)
    def _(i):
        at = cols(i)
        inner[:, at] = dot(h_two[...], w_first[:, at]) + wide_ref[0:1, at]

    @pl.loop(0, seq // group)
    def _(i):
        at = cols(i, group)
        a = inner[at, :]
        cdf = 0.5 * (1.0 + lax.erf(a * (1.0 / math.sqrt(2.0))))
        inner[at, :] = cdf + a * jnp.exp(-0.5 * a * a) * (1.0 / math.sqrt(2.0 * math.pi))
        hat, inverse = row_norm(a * cdf)
        hat_inner[at, :] = hat
        stats[at, 2:3] = inverse
        hidden[at, :] = (hat * wide(1) + wide(2)).astype(bf16)

    fetches[2].wait()

    @pl.loop(0, deep // chunk)
    def _(i):
        at = cols(i)
        g_second[at, :] = dot(hidden[:, at], cot_ref[...], TN).astype(bf16)
        d_hidden[:, at] = dot(cot_ref[...], w_second[at, :], NT)

    outs = [pltpu.make_async_copy(src, dst, out_sem.at[i]) for i, (src, dst) in enumerate(
        ((g_out, g_out_hbm), (g_first, g_first_hbm), (g_second, g_second_hbm)))]
    outs[2].start()

    @pl.loop(0, width // chunk)
    def _(i):
        at = cols(i)
        output_ref[:, at] = (first[:, at] + (dot(hidden[...], w_second[:, at]) + narrow_ref[7:8, at])).astype(bf16)

    @pl.loop(0, seq // group)
    def _(i):
        at = cols(i, group)
        grad, hat = d_hidden[at, :], hat_inner[at, :]
        acc_w[8:16, :] += folded(grad * hat)
        acc_w[16:24, :] += folded(grad)
        da = (row_back(grad, hat, stats[at, 2:3], wide(1)) * inner[at, :]).astype(bf16)
        hidden[at, :] = da
        acc_w[0:8, :] += folded(da.astype(f32))

    h_two_t[...] = h_two[...].T

    @pl.loop(0, deep // chunk)
    def _(i):
        at = cols(i)
        g_first[:, at] = dot(h_two_t[...], hidden[:, at]).astype(bf16)

    outs[1].start()

    @pl.loop(0, seq // half)
    def _(i):
        at = cols(i, half)
        d_two = dot(hidden[at, :], w_first[...], NT)
        hat = hat_two[at, :]
        cot = cot_ref[at, :].astype(f32)
        d_x1 = cot + row_back(d_two, hat, stats[at, 1:2], narrow(5))
        d_first_ref[at, :] = d_x1
        post = hat_post[at, :]
        dz = row_back(d_x1, post, stats[at, 0:1], narrow(3)).astype(bf16)
        d_mixed[at, :] = dz
        du = dot(dz, w_out[...], NT)
        d_attn_ref[at, :] = (du * scale_ref[...]).astype(bf16)
        for row, value in ((2, dz.astype(f32)), (3, d_x1 * post), (4, d_x1), (5, d_two * hat), (6, d_two), (7, cot),
                           (0, du * attn_ref[at, :])):
            acc_n[8 * row : 8 * row + 8, :] += folded(value)

    g_out[...] = dot(scaled[...], d_mixed[...], TN).astype(bf16)
    outs[0].start()
    for row in range(8):
        narrow_out[row : row + 1, :] = jnp.sum(acc_n[8 * row : 8 * row + 8, :], axis=0, keepdims=True)
    wide_out[...] = jnp.zeros_like(wide_out)
    for row in range(3):
        wide_out[row : row + 1, :] = jnp.sum(acc_w[8 * row : 8 * row + 8, :], axis=0, keepdims=True)
    for out in outs:
        out.wait()


def middle(attn, tokens, cotangent, scale, narrow, wide, w_out, w_first, w_second):
    seq, width = tokens.shape
    deep = w_first.shape[1]
    vmem, anywhere = pl.BlockSpec(memory_space=pltpu.VMEM), pl.BlockSpec(memory_space=pl.ANY)
    big, tall = (seq, deep), (seq, width)
    return pl.pallas_call(
        middle_kernel,
        in_specs=[vmem] * 6 + [anywhere] * 3,
        out_specs=[vmem] * 3 + [anywhere] * 3 + [vmem] * 2,
        out_shape=[
            jax.ShapeDtypeStruct(tall, bf16), jax.ShapeDtypeStruct(tall, f32), jax.ShapeDtypeStruct(tall, bf16),
            jax.ShapeDtypeStruct(w_out.shape, bf16), jax.ShapeDtypeStruct(w_first.shape, bf16),
            jax.ShapeDtypeStruct(w_second.shape, bf16),
            jax.ShapeDtypeStruct((8, width), f32), jax.ShapeDtypeStruct((8, deep), f32),
        ],
        scratch_shapes=[
            pltpu.VMEM(w_out.shape, bf16), pltpu.VMEM(w_first.shape, bf16), pltpu.VMEM(w_second.shape, bf16),
            pltpu.VMEM(tall, bf16), pltpu.VMEM(tall, f32), pltpu.VMEM((seq, 8), f32), pltpu.VMEM(tall, f32),
            pltpu.VMEM(tall, f32), pltpu.VMEM(tall, bf16), pltpu.VMEM((width, seq), bf16),
            pltpu.VMEM(big, f32), pltpu.VMEM(big, f32), pltpu.VMEM(big, bf16), pltpu.VMEM(big, f32),
            pltpu.VMEM(tall, bf16),
            pltpu.VMEM(w_out.shape, bf16), pltpu.VMEM(w_first.shape, bf16), pltpu.VMEM(w_second.shape, bf16),
            pltpu.VMEM((64, width), f32), pltpu.VMEM((24, deep), f32),
            pltpu.SemaphoreType.DMA((3,)), pltpu.SemaphoreType.DMA((3,)),
        ],
        compiler_params=pltpu.CompilerParams(vmem_limit_bytes=67043328),
        name="middle",
    )(attn, tokens, cotangent, scale, narrow, wide, w_out, w_first, w_second)

AXES = ("wide", "narrow")


def standardize(v):
    centred = v - jnp.mean(v, axis=-1, keepdims=True)
    inverse = lax.rsqrt(jnp.mean(centred * centred, axis=-1, keepdims=True) + 1e-05)
    return centred * inverse, inverse


def norm_back(grad, normed, inverse, gain):
    scaled = grad * gain
    return inverse * (
        scaled
        - jnp.mean(scaled, axis=-1, keepdims=True)
        - normed * jnp.mean(scaled * normed, axis=-1, keepdims=True)
    )


def whole_of(x):
    return lax.all_gather(x, AXES, axis=0, tiled=True)


def share_of(x):
    return lax.psum_scatter(x, AXES, scatter_dimension=0, tiled=True)


def local(devices, direct, tokens, cotangent, segments, buckets, norm1_gain, norm1_bias, qkv_weight, qv_bias,
          head_scale, rel_table, out_weight, out_bias, post_gain, post_bias, norm2_gain, norm2_bias,
          fc1_weight, fc1_bias, inner_gain, inner_bias, fc2_weight, fc2_bias):
    seq, width = tokens.shape
    heads = head_scale.shape[0]
    size = width // heads
    small = (norm1_gain, norm1_bias, out_bias, post_gain, post_bias, norm2_gain, norm2_bias, fc2_bias,
             qv_bias, fc1_bias, inner_gain, inner_bias)
    sizes = [v.shape[0] for v in small]
    nb = rel_table.shape[0] * devices
    scale = jnp.repeat(head_scale.astype(f32), size)[None, :]
    if direct:
        attn, probs, qkv, h_one, narrow, wide, (w_qkv, w_out, w_first, w_second) = forward_all(
            small, rel_table, (qkv_weight, out_weight, fc1_weight, fc2_weight), tokens, buckets, segments)
        output, d_first, d_attn, g_out, g_first, g_second, narrow_sums, wide_sums = middle(
            attn, tokens, cotangent, scale, narrow, wide, w_out, w_first, w_second)
        grad_tokens, *sums, tile, block = backward_all(
            qkv, d_attn, attn, probs, buckets, tokens, h_one, d_first, narrow[0:1], w_qkv,
            (g_second, g_first, g_out), narrow_sums, wide_sums, heads)
        (g_second, g_first, g_out, g_qkv, grad_tokens), grads, g_table, g_scale = finish(
            tile, block, [*sums, grad_tokens], sizes, heads)
        return ordered(output, grad_tokens, grads, g_table, g_scale, g_qkv, g_out, g_first, g_second)
    vectors = [whole_of(v).astype(f32) for v in small]
    table_t = whole_of(rel_table).astype(f32).T.reshape(heads // 2, 2, nb)
    w_qkv, w_out, w_first, w_second = [whole_of(w) for w in (qkv_weight, out_weight, fc1_weight, fc2_weight)]
    (gain_one, bias_one, bias_out, gain_post, bias_post, gain_two, bias_two, bias_second,
     bias_qv, bias_first, gain_inner, bias_inner) = vectors

    inputs = tokens.astype(f32)
    hat_one, inv_one = standardize(inputs)
    h_one = (hat_one * gain_one + bias_one).astype(bf16)
    shift = jnp.concatenate([bias_qv[:width], jnp.zeros((width,), f32), bias_qv[width:]])
    qkv = (dot(h_one, w_qkv) + shift).astype(bf16)
    attn, probs = attention_forward(qkv, table_t, buckets, segments)
    scaled = (attn * scale).astype(bf16)
    mixed = dot(scaled, w_out) + bias_out
    hat_post, inv_post = standardize(mixed)
    first = inputs + hat_post * gain_post + bias_post
    hat_two, inv_two = standardize(first)
    h_two = (hat_two * gain_two + bias_two).astype(bf16)
    inner = dot(h_two, w_first) + bias_first
    cdf = 0.5 * (1.0 + lax.erf(inner * (1.0 / math.sqrt(2.0))))
    hat_inner, inv_inner = standardize(inner * cdf)
    hidden = (hat_inner * gain_inner + bias_inner).astype(bf16)
    output = (first + (dot(hidden, w_second) + bias_second)).astype(bf16)

    grad_out = cotangent.astype(f32)
    g_second = dot(hidden, cotangent, TN)
    g_second_bias = jnp.sum(grad_out, axis=0)
    d_hidden = dot(cotangent, w_second, NT)
    g_inner_gain = jnp.sum(d_hidden * hat_inner, axis=0)
    g_inner_bias = jnp.sum(d_hidden, axis=0)
    d_gelu = norm_back(d_hidden, hat_inner, inv_inner, gain_inner)
    pdf = jnp.exp(-0.5 * inner * inner) * (1.0 / math.sqrt(2.0 * math.pi))
    d_inner = (d_gelu * (cdf + inner * pdf)).astype(bf16)
    g_first_bias = jnp.sum(d_inner.astype(f32), axis=0)
    g_first = dot(h_two, d_inner, TN)
    d_two = dot(d_inner, w_first, NT)
    g_two_gain = jnp.sum(d_two * hat_two, axis=0)
    g_two_bias = jnp.sum(d_two, axis=0)
    d_first = grad_out + norm_back(d_two, hat_two, inv_two, gain_two)
    g_post_gain = jnp.sum(d_first * hat_post, axis=0)
    g_post_bias = jnp.sum(d_first, axis=0)
    d_mixed = norm_back(d_first, hat_post, inv_post, gain_post).astype(bf16)
    g_out_bias = jnp.sum(d_mixed.astype(f32), axis=0)
    g_out = dot(scaled, d_mixed, TN)
    d_scaled = dot(d_mixed, w_out, NT)
    g_scale = jnp.sum(jnp.sum(d_scaled * attn, axis=0).reshape(heads, size), axis=1)
    d_attn = (d_scaled * scale).astype(bf16)
    dq, dk, dv, hist = attention_backward(qkv, d_attn, attn, probs, buckets, nb)
    dqkv = jnp.concatenate([dq, dk, dv], axis=1)
    g_qv = jnp.concatenate([jnp.sum(dq.astype(f32), axis=0), jnp.sum(dv.astype(f32), axis=0)])
    d_one = dot(dqkv, w_qkv, NT)
    g_one_gain = jnp.sum(d_one * hat_one, axis=0)
    g_one_bias = jnp.sum(d_one, axis=0)
    grad_tokens = (d_first + norm_back(d_one, hat_one, inv_one, gain_one)).astype(bf16)
    g_second, g_first, g_out, g_qkv = [share_of(g) for g in (g_second, g_first, g_out, dot(h_one, dqkv, TN))]
    grads = [share_of(g) for g in (
        g_one_gain, g_one_bias, g_out_bias, g_post_gain, g_post_bias, g_two_gain, g_two_bias,
        g_second_bias, g_qv, g_first_bias, g_inner_gain, g_inner_bias)]
    g_table = share_of(table_gradient(hist, heads))
    g_scale = lax.psum(g_scale, AXES)
    return ordered(output, grad_tokens, grads, g_table, g_scale, g_qkv, g_out, g_first, g_second)


def ordered(output, grad_tokens, grads, g_table, g_scale, g_qkv, g_out, g_first, g_second):
    (g_one_gain, g_one_bias, g_out_bias, g_post_gain, g_post_bias, g_two_gain, g_two_bias,
     g_second_bias, g_qv, g_first_bias, g_inner_gain, g_inner_bias) = grads
    return (output, grad_tokens, g_one_gain, g_one_bias, g_qkv, g_qv, g_scale, g_table, g_out, g_out_bias,
            g_post_gain, g_post_bias, g_two_gain, g_two_bias, g_first, g_first_bias, g_inner_gain,
            g_inner_bias, g_second, g_second_bias)


def solution(mesh):
    devices = mesh.shape["wide"] * mesh.shape["narrow"]
    direct = (mesh.shape["wide"], mesh.shape["narrow"]) == (8, 4)
    split, line, whole = P(AXES, None), P(AXES), P()
    return jax.shard_map(
        functools.partial(local, devices, direct),
        mesh=mesh,
        in_specs=(split, split, split, whole, line, line, split, line, whole, split, split, line, line,
                  line, line, line, split, line, line, line, split, line),
        out_specs=(split, split, line, line, split, line, whole, split, split, line, line, line, line,
                   line, split, line, line, line, split, line),
        check_vma=False,
    )
```
